128 devices in a mesh: tm: 2 (over core), space: 64 (over z, y, x).
Axes of the slice: x: 4, y: 4, z: 4, core: 2. Of those that a mesh axis runs over, the one named last changes fastest.
Arguments:
- initial: float32 [256, 64, 128], P('space'), may hold values from -6 to 6
- guess: float32 [8, 256, 64, 128], P('tm', 'space'), may hold values from -6 to 6
- conduct: float32 [256, 64, 128], P('space'), may hold values from 0.3 to 3
- source: float32 [256, 64, 128], P('space'), may hold values from -6 to 6
- profile: float32 [64], P('tm'), may hold values from -1 to 1
Outputs:
- corrected: float32 [8, 256, 64, 128], P('tm', 'space')
- residual: float32 [8, 256, 64, 128], P('tm', 'space')
The draws below stay inside these ranges and needn't reach their ends.
All inputs are finite; a program needn't handle non-finite values.
Results may differ from the reference program's by a relative error of at most 0.000048.
Values sent between devices are 32-bit elements; how exact they have to be, the bound alone decides.
A program may use at most 64 MiB of HBM per device.

```python
import math
import jax
import jax.numpy as jnp

NX = 64
NY = 128
COARSEN = 8
SWEEPS = 3
NZ = 256
INTERVALS = 8
STEPS = 64


def block_levels(own_key, extent, pieces, least, largest):
    level, own = 1.0, jax.random.fold_in(own_key, 6)
    for dim, parts in pieces:
        heights = jnp.exp(jax.random.uniform(jax.random.fold_in(own, dim), (parts,), jnp.float32, least / len(pieces), largest / len(pieces)))
        level = level * jnp.repeat(heights, extent[dim] // parts).reshape([-1 if axis == dim else 1 for axis in range(len(extent))])
    return level


def bell_draw(key, extent, deviation, limit, shards=(), kind=jnp.bfloat16):
    loudness = block_levels(key, extent, shards, -0.22, 0.18) if shards else 1.0
    array = jax.random.normal(key, extent, jnp.float32) * deviation * loudness
    return jnp.minimum(jnp.maximum(array, -limit), limit).astype(kind)


def setup_inputs(seed: int = 0) -> dict:
    splits = jax.random.split(jax.random.key(seed), 6)
    return {
        "initial": bell_draw(splits[0], (NZ, NX, NY), 1.0, 6.0, ((0, 64),), jnp.float32),
        "guess": bell_draw(splits[1], (INTERVALS, NZ, NX, NY), 1.0, 6.0, ((0, 2), (1, 64)), jnp.float32),
        "conduct": jnp.clip(jnp.exp(math.log(3.0) - 2.3025851 * jax.random.uniform(splits[2], (NZ, NX, NY), jnp.float32) ** block_levels(splits[2], (NZ, NX, NY), ((0, 64),), -0.2, 0.2)), 0.3, 3.0),
        "source": bell_draw(splits[3], (NZ, NX, NY), 1.0, 6.0, ((0, 64),), jnp.float32),
        "profile": jnp.clip(jax.random.uniform(splits[4], (STEPS,), jnp.float32, -1.0, 1.0) * block_levels(splits[4], (STEPS,), ((0, 2),), -0.4, 0.0), -1.0, 1.0),
    }


KAPPA_TOP = 3.0


def laplace(field):
    padded = jnp.pad(field, ((0, 0), (1, 1), (1, 1), (1, 1)))
    centre = padded[:, 1:-1, 1:-1, 1:-1]
    beside = padded[:, 2:, 1:-1, 1:-1] + padded[:, :-2, 1:-1, 1:-1]
    beside = beside + padded[:, 1:-1, 2:, 1:-1] + padded[:, 1:-1, :-2, 1:-1]
    beside = beside + padded[:, 1:-1, 1:-1, 2:] + padded[:, 1:-1, 1:-1, :-2]
    return 6.0 * centre - beside


def advance(start, amount, conduct, source, scale, top):
    middle = (top + 1.0) / 2.0
    spread = (top - 1.0) / 2.0
    relative = middle / spread
    ratio_now = 1.0 / relative
    remain = amount * source - scale * conduct * laplace(start)
    update = remain / middle
    iterate = start + update
    for sweep in range(SWEEPS - 1):
        remain = remain - (update + scale * conduct * laplace(update))
        ratio_next = 1.0 / (2.0 * relative - ratio_now)
        update = ratio_next * ratio_now * update + (2.0 * ratio_next / spread) * remain
        iterate = iterate + update
        ratio_now = ratio_next
    return iterate


def reference(initial, guess, conduct, source, profile):
    amounts = profile.reshape(INTERVALS, COARSEN)
    fine_top = 1.0 + 12.0 * KAPPA_TOP
    coarse_top = 1.0 + 12.0 * KAPPA_TOP * COARSEN

    def sweep_interval(entry):
        state = entry
        for inner in range(COARSEN):
            state = advance(state, amounts[:, inner][:, None, None, None], conduct, source, 1.0, fine_top)
        return state

    entry = jnp.concatenate([initial[None], guess[:-1]], axis=0)
    relaxed = sweep_interval(entry)
    again = jnp.concatenate([initial[None], relaxed[:-1]], axis=0)
    residual = sweep_interval(again) - relaxed
    nothing = jnp.zeros((1, 1, 1, 1), jnp.float32)
    error = jnp.zeros_like(initial)
    collected = []
    for section in range(INTERVALS):
        error = advance(error[None], nothing, conduct, source, float(COARSEN), coarse_top)[0] + residual[section]
        collected.append(error)
    corrected = relaxed + jnp.stack(collected, axis=0)
    return corrected, residual
```

```python
import numpy as np
import jax
import jax.numpy as jnp
from jax import lax
from jax.experimental import pallas as pl
from jax.experimental.pallas import tpu as pltpu
from jax.sharding import PartitionSpec as P

SWEEPS = 3
KAPPA_TOP = 3.0
COARSEN = 8
H = 6
B = 16
LT = B + 2 * H
GROUPS = COARSEN * SWEEPS // H
CH = 3
CT = 4 + 2 * CH
F32 = jnp.float32
MESH = pl.DeviceIdType.MESH


def polynomials(scale, top):
    middle, spread = (top + 1.0) / 2.0, (top - 1.0) / 2.0
    relative = middle / spread
    ratio = 1.0 / relative
    one = np.polynomial.Polynomial([1.0])
    system = np.polynomial.Polynomial([1.0, scale])
    remain = one
    update = remain / middle
    total = update
    for _ in range(SWEEPS - 1):
        remain = remain - system * update
        following = 1.0 / (2.0 * relative - ratio)
        update = following * ratio * update + 2.0 * following / spread * remain
        total = total + update
        ratio = following
    rest = one - np.polynomial.Polynomial([0.0, scale]) * total
    return [float(r) for r in np.sort(rest.roots().real)], [float(c) for c in total.coef]


FINE_ROOTS, FINE_P = polynomials(1.0, 1.0 + 12.0 * KAPPA_TOP)
COARSE_ROOTS, _ = polynomials(float(COARSEN), 1.0 + 12.0 * KAPPA_TOP * COARSEN)


class Masks:
    def __init__(self):
        lane = lax.broadcasted_iota(jnp.int32, (8, 8, 128), 2)
        sub = lax.broadcasted_iota(jnp.int32, (8, 128), 0)
        self.first_lane, self.last_lane = lane == 0, lane == 127
        self.first_sub, self.last_sub = sub == 0, sub == 7


def neighbours(below, centre, above, mk):
    side = jnp.where(mk.first_lane, 0.0, pltpu.roll(centre, 1, 2))
    side = side + jnp.where(mk.last_lane, 0.0, pltpu.roll(centre, 127, 2))
    before = jnp.where(mk.first_sub, 0.0, pltpu.roll(centre[7], 1, 0))
    after = jnp.where(mk.last_sub, 0.0, pltpu.roll(centre[0], 7, 0))
    rows = jnp.concatenate([before[None], centre[:7]], axis=0) + jnp.concatenate(
        [centre[1:], after[None]], axis=0
    )
    return (side + rows) + (below + above)


def natural(ref, layer):
    return jnp.stack([ref[layer, pl.ds(j, 8, stride=8), :] for j in range(8)], axis=0)


def kernel(
    initial, guess, conduct, source, amount,
    corrected, residual,
    nat, con_nat, prof, kap, mul, grow, ua, ub, land, stage, rel, kc, mc, eb, t1, t2, res_in, rel_in,
    in_send, in_recv, nat_send, nat_recv, prof_sem, con_sem, halo_send, halo_recv,
    out_send, out_recv, chain_send, chain_recv,
):
    m = lax.axis_index("tm")
    c = lax.axis_index("space")
    mk = Masks()

    x, y, z = c % 4, (c // 4) % 4, c // 16
    half = y // 2
    s = jnp.where(half == 0, y, 3 - y)
    k = x + 4 * half
    q = 2 * (2 * z + (s + z) % 2) + m

    def device(kk, qq):
        b = qq // 2
        zz = b // 2
        ss = (b % 2 + zz % 2) % 2
        yy = jnp.where(kk // 4 == 0, ss, 3 - ss)
        return (qq % 2, zz * 16 + yy * 4 + kk % 4)

    def remote(src, dst, ssem, rsem, to):
        return pltpu.make_async_remote_copy(
            src_ref=src, dst_ref=dst, send_sem=ssem, recv_sem=rsem, device_id=to, device_id_type=MESH
        )

    def is_me(to):
        return jnp.logical_and(to[0] == m, to[1] == c)

    def push(src, dst, ssem, rsem, to):
        mine = is_me(to)

        @pl.when(mine)
        def _():
            pltpu.make_async_copy(src, dst, rsem).start()

        @pl.when(jnp.logical_not(mine))
        def _():
            remote(src, dst, ssem, rsem, to).start()

    def pushed(src, dst, ssem, rsem, to):
        @pl.when(jnp.logical_not(is_me(to)))
        def _():
            remote(src, dst, ssem, rsem, to).wait_send()

    def arrived(dst, rsem):
        pltpu.make_async_copy(dst, dst, rsem).wait()

    sq, sr = c // 4, c % 4
    place = pl.ds(H + 4 * sr, 4)
    own = pl.ds(H, B)
    sends = []

    def give(array, slot, src, kk, when=None):
        args = (src, nat.at[array, place], in_send.at[array, slot], in_recv.at[array, sr], device(kk, sq))
        sends.append((args, when))
        if when is None:
            push(*args)
        else:
            pl.when(when)(lambda: push(*args))

    chain_left, chain_right = (m, c - 1), (m, c + 1)
    has_cl, has_cr = c > 0, c < 63
    con_local = pltpu.make_async_copy(conduct, con_nat.at[pl.ds(CH, 4)], con_sem.at[0])
    to_cl = remote(conduct.at[pl.ds(0, CH)], con_nat.at[pl.ds(CH + 4, CH)], con_sem.at[1], con_sem.at[2], chain_left)
    to_cr = remote(conduct.at[pl.ds(1, CH)], con_nat.at[pl.ds(0, CH)], con_sem.at[3], con_sem.at[4], chain_right)

    partner = (1 - m, c)
    to_partner = remote(amount, prof.at[pl.ds(4 * m, 4)], prof_sem.at[0], prof_sem.at[1], partner)
    mine_prof = pltpu.make_async_copy(amount, prof.at[pl.ds(4 * m, 4)], prof_sem.at[2])

    for i in range(4):
        give(0, i, conduct, 4 * m + i)
    pl.when(m == 0)(lambda: push(initial, nat.at[1, place], in_send.at[1, 4], in_recv.at[1, sr], device(0, sq)))
    for i in range(3):
        give(1, i, guess.at[i], 4 * m + i + 1)
    give(1, 3, guess.at[3], 4, m == 0)
    for i in range(4):
        give(2, i, source, 4 * m + i)
    to_partner.start()
    mine_prof.start()
    for i in range(3):
        give(3, i, guess.at[i], 4 * m + i)
    give(3, 3, guess.at[3], 3, m == 0)
    pl.when(m == 1)(lambda: push(initial, nat.at[3, place], in_send.at[3, 4], in_recv.at[3, sr], device(7, sq)))
    con_local.start()
    pl.when(has_cl)(lambda: to_cl.start())
    pl.when(has_cr)(lambda: to_cr.start())

    left, right = device(k, jnp.maximum(q - 1, 0)), device(k, jnp.minimum(q + 1, 15))
    has_l, has_r = q > 0, q < 15
    nat_copies = []
    for array in range(3):
        to_l = remote(
            nat.at[array, pl.ds(H, H)], nat.at[array, pl.ds(H + B, H)],
            nat_send.at[0, array], nat_recv.at[0, array], left,
        )
        to_r = remote(
            nat.at[array, pl.ds(B, H)], nat.at[array, pl.ds(0, H)],
            nat_send.at[1, array], nat_recv.at[1, array], right,
        )
        nat_copies.append((to_l, to_r))
        for r in range(2):
            arrived(nat.at[array, pl.ds(H + 4 * r, 4)], in_recv.at[array, r])
        pl.when(has_l)(lambda: to_l.start())
        for r in range(2, 4):
            arrived(nat.at[array, pl.ds(H + 4 * r, 4)], in_recv.at[array, r])
        pl.when(has_r)(lambda: to_r.start())

    def halo_arrived(array):
        pl.when(has_r)(lambda: arrived(nat.at[array, pl.ds(H + B, H)], nat_recv.at[0, array]))
        pl.when(has_l)(lambda: arrived(nat.at[array, pl.ds(0, H)], nat_recv.at[1, array]))

    def coefficients(layer, cond):
        for n in range(3):
            kappa = cond * (1.0 / FINE_ROOTS[n])
            kap[n, layer] = kappa
            mul[n, layer] = 1.0 - 6.0 * kappa
        kap[3, layer] = cond

    nothing = jnp.zeros((8, 8, 128), F32)

    def edges(has, first, fill, blank):
        @pl.when(has)
        def _():
            @pl.loop(first, first + H)
            def _(layer):
                fill(layer)

        @pl.when(jnp.logical_not(has))
        def _():
            @pl.loop(first, first + H)
            def _(layer):
                blank(layer)

    def fill_con(layer):
        coefficients(layer, natural(nat.at[0], layer))

    def blank_con(layer):
        for n in range(3):
            kap[n, layer] = nothing
            mul[n, layer] = nothing
        kap[3, layer] = nothing

    def fill_src(layer):
        ub[layer] = natural(nat.at[2], layer)

    def blank_src(layer):
        ub[layer] = nothing

    @pl.loop(H, H + B)
    def _(layer):
        fill_con(layer)

    halo_arrived(0)
    edges(has_l, 0, fill_con, blank_con)
    edges(has_r, H + B, fill_con, blank_con)

    @pl.loop(H, H + B)
    def _(layer):
        fill_src(layer)

    halo_arrived(2)
    edges(has_l, 0, fill_src, blank_src)
    edges(has_r, H + B, fill_src, blank_src)

    def applied(ref, layer):
        centre = ref[layer]
        return kap[3, layer] * (6.0 * centre - neighbours(ref[layer - 1], centre, ref[layer + 1], mk))

    @pl.loop(1, LT - 1)
    def _(layer):
        ua[layer] = FINE_P[1] * ub[layer] + FINE_P[2] * applied(ub, layer)

    @pl.loop(2, LT - 2)
    def _(layer):
        grow[layer] = FINE_P[0] * ub[layer] + applied(ua, layer)

    @pl.loop(H, H + B)
    def _(layer):
        ua[layer] = natural(nat.at[1], layer)

    halo_arrived(1)
    for side, has, first in ((0, has_l, 0), (1, has_r, H + B)):
        def fill(layer, side=side, first=first):
            land[0, side, layer - first] = natural(nat.at[1], layer)

        def blank(layer, side=side, first=first):
            land[0, side, layer - first] = nothing
            land[1, side, layer - first] = nothing

        edges(has, first, fill, blank)

    arrived(prof.at[pl.ds(4 * (1 - m), 4)], prof_sem.at[1])
    mine_prof.wait()

    def state_copies(t):
        p = t % 2
        return (
            remote(stage.at[p, 0], land.at[p, 1], halo_send.at[0, p], halo_recv.at[0, p], left),
            remote(stage.at[p, 1], land.at[p, 0], halo_send.at[1, p], halo_recv.at[1, p], right),
        )

    def group(g, with_source):
        parity = g % 2
        following = (g + 1) % 2
        bufs = (ua, ub)

        def read(i, layer):
            if i == 0 and layer < H:
                return land[parity, 0, layer]
            if i == 0 and layer >= H + B:
                return land[parity, 1, layer - H - B]
            return bufs[i % 2][layer]

        amounts = {}
        if with_source:
            for n in range(H // 3):
                row = prof[k, pl.ds(g * (H // 3) + n, 1), :]
                amounts[3 * n + 3] = jnp.broadcast_to(row, (8, 128))

        def region(bounds, sent=None):
            todo = []
            for i in range(1, H + 1):
                lo, hi = bounds(i)
                todo += [(layer + 2 * i, i, layer) for layer in range(lo, hi)]
            for _, i, layer in sorted(todo):
                n = (i - 1) % 3
                centre = read(i - 1, layer)
                total = neighbours(read(i - 1, layer - 1), centre, read(i - 1, layer + 1), mk)
                value = mul[n, layer] * centre + kap[n, layer] * total
                if i in amounts:
                    value = value + amounts[i][None] * grow[layer]
                bufs[i % 2][layer] = value
                if i == H and sent is not None:
                    stage[following, sent[0], layer - sent[1]] = value

        @pl.when(g >= 2)
        def _():
            a, b = state_copies(g + 1)
            pl.when(has_l)(lambda: a.wait_send())
            pl.when(has_r)(lambda: b.wait_send())

        region(lambda i: (H + i, H + B - i))
        a, b = state_copies(g)
        c_, d_ = state_copies(g + 1)
        last = COARSEN * SWEEPS // H

        @pl.when(jnp.logical_and(g > 0, has_l))
        def _():
            b.wait_recv()

        region(lambda i: (i, H + i), (0, H))

        @pl.when(jnp.logical_and((g + 1) % last != 0, has_l))
        def _():
            c_.start()

        @pl.when(jnp.logical_and(g > 0, has_r))
        def _():
            a.wait_recv()

        region(lambda i: (LT - H - i, LT - i), (1, B))

        @pl.when(jnp.logical_and((g + 1) % last != 0, has_r))
        def _():
            d_.start()

    @pl.loop(0, GROUPS)
    def _(g):
        group(g, True)

    for r in range(4):
        arrived(nat.at[3, pl.ds(H + 4 * r, 4)], in_recv.at[3, r])
    first_copies = state_copies(GROUPS)
    final = k == 7

    def difference(layer):
        value = ua[layer]
        off = natural(nat.at[3], layer)
        rel[layer - H] = value
        value = jnp.where(final, off, value) - off
        ua[layer] = value
        return value

    @pl.loop(0, H)
    def _(i):
        stage[GROUPS % 2, 0, i] = difference(H + i)

    pl.when(has_l)(lambda: first_copies[0].start())

    @pl.loop(2 * H, B)
    def _(layer):
        difference(layer)

    @pl.loop(0, H)
    def _(i):
        stage[GROUPS % 2, 1, i] = difference(B + i)

    pl.when(has_r)(lambda: first_copies[1].start())

    after = (k + 1) % 8
    rel_args = [
        (rel.at[pl.ds(4 * r, 4)], rel_in.at[k % 4], out_send.at[0, r], out_recv.at[0, k % 4], (k // 4, 4 * q + r))
        for r in range(4)
    ]
    res_args = [
        (ua.at[pl.ds(H + 4 * r, 4)], res_in.at[after % 4], out_send.at[1, r], out_recv.at[1, after % 4], (after // 4, 4 * q + r))
        for r in range(4)
    ]
    for args in rel_args:
        push(*args)

    @pl.loop(GROUPS, 2 * GROUPS)
    def _(g):
        group(g, False)

    for args in res_args:
        push(*args)

    con_local.wait()
    pl.when(has_cl)(lambda: to_cr.wait_recv())
    pl.when(has_cr)(lambda: to_cl.wait_recv())

    def chain_fill(layer):
        cond = natural(con_nat, layer)
        for n in range(3):
            kappa = cond * (1.0 / COARSE_ROOTS[n])
            kc[n, layer] = kappa
            mc[n, layer] = 1.0 - 6.0 * kappa

    for layer in range(CH, CH + 4):
        chain_fill(layer)
    for has, first in ((has_cl, 0), (has_cr, CH + 4)):
        @pl.when(has)
        def _(first=first):
            for layer in range(first, first + CH):
                chain_fill(layer)

        @pl.when(jnp.logical_not(has))
        def _(first=first):
            for layer in range(first, first + CH):
                for n in range(3):
                    kc[n, layer] = nothing
                    mc[n, layer] = nothing
                eb[0, layer] = nothing
                eb[1, layer] = nothing

    def out_rows(ref, i, layer, value):
        for j in range(8):
            ref[i, layer, pl.ds(j, 8, stride=8), :] = value[j]

    def chain_copies(i):
        p = i % 2
        core = jnp.where(i == 3, 1, m)
        lft, rgt = (core, c - 1), (core, c + 1)
        return (
            remote(eb.at[p, pl.ds(CH, CH)], eb.at[p, pl.ds(CH + 4, CH)], chain_send.at[0, p], chain_recv.at[0, p], lft),
            remote(eb.at[p, pl.ds(4, CH)], eb.at[p, pl.ds(0, CH)], chain_send.at[1, p], chain_recv.at[1, p], rgt),
        )

    over = remote(eb.at[1, pl.ds(CH, 4)], eb.at[1, pl.ds(CH, 4)], chain_send.at[2, 0], chain_recv.at[2, 0], (1, c))

    @pl.loop(0, 4)
    def _(i):
        p = i % 2
        o = 1 - p
        arrived(res_in.at[i], out_recv.at[1, i])
        start = jnp.logical_and(m == 0, i == 0)

        @pl.when(start)
        def _():
            for layer in range(4):
                eb[p, CH + layer] = res_in[i, layer]

        @pl.when(jnp.logical_not(start))
        def _():
            a, b = chain_copies(i + 1)
            pl.when(has_cr)(lambda: a.wait_recv())
            pl.when(has_cl)(lambda: b.wait_recv())
            pl.when(i == 0)(lambda: over.wait_recv())

            @pl.when(i >= 2)
            def _():
                d, e = chain_copies(i - 2)
                pl.when(has_cl)(lambda: d.wait_send())
                pl.when(has_cr)(lambda: e.wait_send())

            src = eb.at[o]
            for n, dst in enumerate((t1, t2, None)):
                for layer in range(n + 1, CT - n - 1):
                    centre = src[layer]
                    total = neighbours(src[layer - 1], centre, src[layer + 1], mk)
                    value = mc[n, layer] * centre + kc[n, layer] * total
                    if dst is None:
                        eb[p, layer] = value + res_in[i, layer - CH]
                    else:
                        dst[layer] = value
                src = dst

        d, e = chain_copies(i)
        more = jnp.logical_or(i < 3, m == 0)
        pl.when(jnp.logical_and(more, has_cl))(lambda: d.start())
        pl.when(jnp.logical_and(more, has_cr))(lambda: e.start())
        pl.when(jnp.logical_and(i == 3, m == 0))(lambda: over.start())
        arrived(rel_in.at[i], out_recv.at[0, i])
        for layer in range(4):
            out_rows(residual, i, layer, res_in[i, layer])
            out_rows(corrected, i, layer, rel_in[i, layer] + eb[p, CH + layer])

    d, e = chain_copies(2)
    pl.when(has_cl)(lambda: d.wait_send())
    pl.when(has_cr)(lambda: e.wait_send())
    d, e = chain_copies(3)

    @pl.when(m == 0)
    def _():
        pl.when(has_cl)(lambda: d.wait_send())
        pl.when(has_cr)(lambda: e.wait_send())
        over.wait_send()

    for args, when in sends:
        if when is None:
            pushed(*args)
        else:
            pl.when(when)(lambda: pushed(*args))
    pl.when(m == 0)(lambda: pushed(initial, nat.at[1, place], in_send.at[1, 4], in_recv.at[1, sr], device(0, sq)))
    pl.when(m == 1)(lambda: pushed(initial, nat.at[3, place], in_send.at[3, 4], in_recv.at[3, sr], device(7, sq)))
    for to_l, to_r in nat_copies:
        pl.when(has_l)(lambda: to_l.wait_send())
        pl.when(has_r)(lambda: to_r.wait_send())
    pl.when(has_cl)(lambda: to_cl.wait_send())
    pl.when(has_cr)(lambda: to_cr.wait_send())
    to_partner.wait_send()
    for args in rel_args + res_args:
        pushed(*args)
    a, b = state_copies(2 * GROUPS - 1)
    pl.when(has_l)(lambda: a.wait_send())
    pl.when(has_r)(lambda: b.wait_send())


def body(initial, guess, conduct, source, profile):
    amount = jnp.broadcast_to(profile.reshape(4, COARSEN, 1), (4, COARSEN, 128))
    anyspace = pl.BlockSpec(memory_space=pl.ANY)
    vmem = pl.BlockSpec(memory_space=pltpu.VMEM)
    out = jax.ShapeDtypeStruct((4, 4, 64, 128), F32)
    dma = pltpu.SemaphoreType.DMA

    def layers(*lead):
        return pltpu.VMEM((*lead, 8, 8, 128), F32)

    return pl.pallas_call(
        kernel,
        name="mgrit",
        out_shape=(out, out),
        in_specs=[anyspace, anyspace, anyspace, anyspace, vmem],
        out_specs=(vmem, vmem),
        scratch_shapes=[
            pltpu.VMEM((4, LT, 64, 128), F32),
            pltpu.VMEM((CT, 64, 128), F32),
            pltpu.VMEM((8, COARSEN, 128), F32),
            layers(4, LT),
            layers(3, LT),
            layers(LT),
            layers(LT),
            layers(LT),
            layers(2, 2, H),
            layers(2, 2, H),
            layers(B),
            layers(3, CT),
            layers(3, CT),
            layers(2, CT),
            layers(CT),
            layers(CT),
            layers(4, 4),
            layers(4, 4),
            dma((4, 5)), dma((4, 4)),
            dma((2, 3)), dma((2, 3)),
            dma((3,)), dma((5,)),
            dma((2, 2)), dma((2, 2)),
            dma((2, 4)), dma((2, 4)),
            dma((3, 2)), dma((3, 2)),
        ],
        compiler_params=pltpu.CompilerParams(has_side_effects=True, vmem_limit_bytes=48 * 1024 * 1024),
    )(initial, guess, conduct, source, amount)


def solution(mesh):
    return jax.shard_map(
        body,
        mesh=mesh,
        in_specs=(
            P("space", None, None),
            P("tm", "space", None, None),
            P("space", None, None),
            P("space", None, None),
            P("tm"),
        ),
        out_specs=(P("tm", "space", None, None), P("tm", "space", None, None)),
        check_vma=False,
    )
```

```python
import numpy as np
import jax
import jax.numpy as jnp
from jax import lax
from jax.experimental import pallas as pl
from jax.experimental.pallas import tpu as pltpu
from jax.sharding import PartitionSpec as P

SWEEPS = 3
KAPPA_TOP = 3.0
COARSEN = 8
H = 6
B = 16
LT = B + 2 * H
GROUPS = COARSEN * SWEEPS // H
CH = 3
CT = 4 + 2 * CH
F32 = jnp.float32
MESH = pl.DeviceIdType.MESH


def polynomials(scale, top):
    middle, spread = (top + 1.0) / 2.0, (top - 1.0) / 2.0
    relative = middle / spread
    ratio = 1.0 / relative
    one = np.polynomial.Polynomial([1.0])
    system = np.polynomial.Polynomial([1.0, scale])
    remain = one
    update = remain / middle
    total = update
    for _ in range(SWEEPS - 1):
        remain = remain - system * update
        following = 1.0 / (2.0 * relative - ratio)
        update = following * ratio * update + 2.0 * following / spread * remain
        total = total + update
        ratio = following
    rest = one - np.polynomial.Polynomial([0.0, scale]) * total
    return [float(r) for r in np.sort(rest.roots().real)], [float(c) for c in total.coef]


FINE_ROOTS, FINE_P = polynomials(1.0, 1.0 + 12.0 * KAPPA_TOP)
COARSE_ROOTS, _ = polynomials(float(COARSEN), 1.0 + 12.0 * KAPPA_TOP * COARSEN)


class Masks:
    def __init__(self):
        lane = lax.broadcasted_iota(jnp.int32, (8, 8, 128), 2)
        sub = lax.broadcasted_iota(jnp.int32, (8, 128), 0)
        self.first_lane, self.last_lane = lane == 0, lane == 127
        self.first_sub, self.last_sub = sub == 0, sub == 7


def neighbours(below, centre, above, mk):
    side = jnp.where(mk.first_lane, 0.0, pltpu.roll(centre, 1, 2))
    side = side + jnp.where(mk.last_lane, 0.0, pltpu.roll(centre, 127, 2))
    before = jnp.where(mk.first_sub, 0.0, pltpu.roll(centre[7], 1, 0))
    after = jnp.where(mk.last_sub, 0.0, pltpu.roll(centre[0], 7, 0))
    rows = jnp.concatenate([before[None], centre[:7]], axis=0) + jnp.concatenate(
        [centre[1:], after[None]], axis=0
    )
    return (side + rows) + (below + above)


def natural(ref, layer):
    return jnp.stack([ref[layer, pl.ds(j, 8, stride=8), :] for j in range(8)], axis=0)


def kernel(
    initial, guess, conduct, source, amount,
    corrected, residual,
    nat, con_nat, prof, kap, mul, grow, ua, ub, land, stage, rel, kc, mc, eb, t1, t2, res_in, rel_in,
    in_send, in_recv, nat_send, nat_recv, prof_sem, con_sem, sub_sem, halo_send, halo_recv,
    out_send, out_recv, chain_send, chain_recv,
):
    m = lax.axis_index("tm")
    c = lax.axis_index("space")
    mk = Masks()

    x, y, z = c % 4, (c // 4) % 4, c // 16
    half = y // 2
    s = jnp.where(half == 0, y, 3 - y)
    k = x + 4 * half
    q = 2 * (2 * z + (s + z) % 2) + m

    def device(kk, qq):
        b = qq // 2
        zz = b // 2
        ss = (b % 2 + zz % 2) % 2
        yy = jnp.where(kk // 4 == 0, ss, 3 - ss)
        return (qq % 2, zz * 16 + yy * 4 + kk % 4)

    def remote(src, dst, ssem, rsem, to):
        return pltpu.make_async_remote_copy(
            src_ref=src, dst_ref=dst, send_sem=ssem, recv_sem=rsem, device_id=to, device_id_type=MESH
        )

    def is_me(to):
        return jnp.logical_and(to[0] == m, to[1] == c)

    def push(src, dst, ssem, rsem, to):
        mine = is_me(to)

        @pl.when(mine)
        def _():
            pltpu.make_async_copy(src, dst, rsem).start()

        @pl.when(jnp.logical_not(mine))
        def _():
            remote(src, dst, ssem, rsem, to).start()

    def pushed(src, dst, ssem, rsem, to):
        @pl.when(jnp.logical_not(is_me(to)))
        def _():
            remote(src, dst, ssem, rsem, to).wait_send()

    def arrived(dst, rsem):
        pltpu.make_async_copy(dst, dst, rsem).wait()

    left, right = device(k, jnp.maximum(q - 1, 0)), device(k, jnp.minimum(q + 1, 15))
    has_l, has_r = q > 0, q < 15
    sq, sr = c // 4, c % 4
    has_cl, has_cr = c > 0, c < 63
    place = pl.ds(H + 4 * sr, 4)
    own = pl.ds(H, B)
    sends = []

    def give(array, slot, src, kk, when=None):
        args = (src, nat.at[array, place], in_send.at[array, slot], in_recv.at[array, sr], device(kk, sq))
        sends.append((args, when))
        if when is None:
            push(*args)
        else:
            pl.when(when)(lambda: push(*args))

    chain_left, chain_right = (m, c - 1), (m, c + 1)
    con_local = pltpu.make_async_copy(conduct, con_nat.at[pl.ds(CH, 4)], con_sem.at[0])
    to_cl = remote(conduct.at[pl.ds(0, CH)], con_nat.at[pl.ds(CH + 4, CH)], con_sem.at[1], con_sem.at[2], chain_left)
    to_cr = remote(conduct.at[pl.ds(1, CH)], con_nat.at[pl.ds(0, CH)], con_sem.at[3], con_sem.at[4], chain_right)

    partner = (1 - m, c)
    to_partner = remote(amount, prof.at[m], prof_sem.at[0], prof_sem.at[1], partner)

    give(0, 0, conduct, x + 4 * m)
    give(2, 0, source, x + 4 * m)
    relays = {}
    for array in (0, 2):
        column = nat.at[array, pl.ds(H + 4 * x, 4)]
        relays[array] = [
            remote(column, column, in_send.at[array, d], in_recv.at[array, x], (m, 16 * z + 4 * y + (x + d) % 4)) for d in range(1, 4)
        ]
        arrived(column, in_recv.at[array, x])
        for relay in relays[array]:
            relay.start()
    pl.when(m == 0)(lambda: push(initial, nat.at[1, place], in_send.at[1, 4], in_recv.at[1, sr], device(0, sq)))
    for i in range(3):
        give(1, i, guess.at[i], 4 * m + i + 1)
    give(1, 3, guess.at[3], 4, m == 0)
    prof[m] = amount[...]

    nat_copies = []

    def beside(array):
        to_l = remote(
            nat.at[array, pl.ds(H, H)], nat.at[array, pl.ds(H + B, H)],
            nat_send.at[0, array], nat_recv.at[0, array], left,
        )
        to_r = remote(
            nat.at[array, pl.ds(B, H)], nat.at[array, pl.ds(0, H)],
            nat_send.at[1, array], nat_recv.at[1, array], right,
        )
        nat_copies.append((to_l, to_r))

        def piece(r):
            def come():
                arrived(nat.at[array, pl.ds(H + 4 * r, 4)], in_recv.at[array, r])

            if array == 1:
                come()
            else:
                pl.when(x != r)(come)

        piece(0)
        piece(1)
        pl.when(has_l)(lambda: to_l.start())
        piece(2)
        piece(3)
        pl.when(has_r)(lambda: to_r.start())

    def halo_arrived(array):
        pl.when(has_r)(lambda: arrived(nat.at[array, pl.ds(H + B, H)], nat_recv.at[0, array]))
        pl.when(has_l)(lambda: arrived(nat.at[array, pl.ds(0, H)], nat_recv.at[1, array]))

    def coefficients(layer, cond):
        for n in range(3):
            kappa = cond * (1.0 / FINE_ROOTS[n])
            kap[n, layer] = kappa
            mul[n, layer] = 1.0 - 6.0 * kappa
        kap[3, layer] = cond

    nothing = jnp.zeros((8, 8, 128), F32)

    def edges(has, first, fill, blank):
        @pl.when(has)
        def _():
            @pl.loop(first, first + H)
            def _(layer):
                fill(layer)

        @pl.when(jnp.logical_not(has))
        def _():
            @pl.loop(first, first + H)
            def _(layer):
                blank(layer)

    def fill_con(layer):
        coefficients(layer, natural(nat.at[0], layer))

    def blank_con(layer):
        for n in range(3):
            kap[n, layer] = nothing
            mul[n, layer] = nothing
        kap[3, layer] = nothing

    def fill_src(layer):
        ub[layer] = natural(nat.at[2], layer)

    def blank_src(layer):
        ub[layer] = nothing

    beside(0)

    @pl.loop(H, H + B)
    def _(layer):
        fill_con(layer)

    beside(2)
    halo_arrived(0)
    edges(has_l, 0, fill_con, blank_con)
    edges(has_r, H + B, fill_con, blank_con)

    @pl.loop(H, H + B)
    def _(layer):
        fill_src(layer)

    halo_arrived(2)
    edges(has_l, 0, fill_src, blank_src)
    edges(has_r, H + B, fill_src, blank_src)

    def applied(ref, layer):
        centre = ref[layer]
        return kap[3, layer] * (6.0 * centre - neighbours(ref[layer - 1], centre, ref[layer + 1], mk))

    @pl.loop(1, LT - 1)
    def _(layer):
        ua[layer] = FINE_P[1] * ub[layer] + FINE_P[2] * applied(ub, layer)

    @pl.loop(2, LT - 2)
    def _(layer):
        grow[layer] = FINE_P[0] * ub[layer] + applied(ua, layer)

    beside(1)
    sub_src, sub_dst = nat.at[1, own], nat.at[3, own]
    sub = remote(sub_src, sub_dst, sub_sem.at[0], sub_sem.at[1], device((k + 7) % 8, q))
    sub.start()
    con_local.start()
    to_partner.start()
    pl.when(has_cl)(lambda: to_cl.start())
    pl.when(has_cr)(lambda: to_cr.start())

    @pl.loop(H, H + B)
    def _(layer):
        ua[layer] = natural(nat.at[1], layer)

    halo_arrived(1)
    for side, has, first in ((0, has_l, 0), (1, has_r, H + B)):
        def fill(layer, side=side, first=first):
            land[0, side, layer - first] = natural(nat.at[1], layer)

        def blank(layer, side=side, first=first):
            land[0, side, layer - first] = nothing
            land[1, side, layer - first] = nothing

        edges(has, first, fill, blank)

    arrived(prof.at[1 - m], prof_sem.at[1])

    def state_copies(t):
        p = t % 2
        return (
            remote(stage.at[p, 0], land.at[p, 1], halo_send.at[0, p], halo_recv.at[0, p], left),
            remote(stage.at[p, 1], land.at[p, 0], halo_send.at[1, p], halo_recv.at[1, p], right),
        )

    def group(g, with_source):
        parity = g % 2
        following = (g + 1) % 2
        bufs = (ua, ub)

        def read(i, layer):
            if i == 0 and layer < H:
                return land[parity, 0, layer]
            if i == 0 and layer >= H + B:
                return land[parity, 1, layer - H - B]
            return bufs[i % 2][layer]

        amounts = {}
        if with_source:
            for n in range(H // 3):
                row = prof[k // 4, pl.ds(COARSEN * (k % 4) + g * (H // 3) + n, 1), :]
                amounts[3 * n + 3] = jnp.broadcast_to(row, (8, 128))

        def region(bounds, sent=None):
            todo = []
            for i in range(1, H + 1):
                lo, hi = bounds(i)
                todo += [(layer + 2 * i, i, layer) for layer in range(lo, hi)]
            for _, i, layer in sorted(todo):
                n = (i - 1) % 3
                centre = read(i - 1, layer)
                total = neighbours(read(i - 1, layer - 1), centre, read(i - 1, layer + 1), mk)
                value = mul[n, layer] * centre + kap[n, layer] * total
                if i in amounts:
                    value = value + amounts[i][None] * grow[layer]
                bufs[i % 2][layer] = value
                if i == H and sent is not None:
                    stage[following, sent[0], layer - sent[1]] = value

        @pl.when(g >= 2)
        def _():
            a, b = state_copies(g + 1)
            pl.when(has_l)(lambda: a.wait_send())
            pl.when(has_r)(lambda: b.wait_send())

        region(lambda i: (H + i, H + B - i))
        a, b = state_copies(g)
        c_, d_ = state_copies(g + 1)
        last = COARSEN * SWEEPS // H

        @pl.when(jnp.logical_and(g > 0, has_l))
        def _():
            b.wait_recv()

        region(lambda i: (i, H + i), (0, H))

        @pl.when(jnp.logical_and((g + 1) % last != 0, has_l))
        def _():
            c_.start()

        @pl.when(jnp.logical_and(g > 0, has_r))
        def _():
            a.wait_recv()

        region(lambda i: (LT - H - i, LT - i), (1, B))

        @pl.when(jnp.logical_and((g + 1) % last != 0, has_r))
        def _():
            d_.start()

    @pl.loop(0, GROUPS)
    def _(g):
        group(g, True)

    arrived(sub_dst, sub_sem.at[1])
    first_copies = state_copies(GROUPS)
    final = k == 7

    def difference(layer):
        value = ua[layer]
        off = natural(nat.at[3], layer)
        rel[layer - H] = value
        value = jnp.where(final, off, value) - off
        ua[layer] = value
        return value

    @pl.loop(0, H)
    def _(i):
        stage[GROUPS % 2, 0, i] = difference(H + i)

    pl.when(has_l)(lambda: first_copies[0].start())

    @pl.loop(2 * H, B)
    def _(layer):
        difference(layer)

    @pl.loop(0, H)
    def _(i):
        stage[GROUPS % 2, 1, i] = difference(B + i)

    pl.when(has_r)(lambda: first_copies[1].start())

    after = (k + 1) % 8
    rel_args = [
        (rel.at[pl.ds(4 * r, 4)], rel_in.at[k % 4], out_send.at[0, r], out_recv.at[0, k % 4], (k // 4, 4 * q + r))
        for r in range(4)
    ]
    res_args = [
        (ua.at[pl.ds(H + 4 * r, 4)], res_in.at[after % 4], out_send.at[1, r], out_recv.at[1, after % 4], (after // 4, 4 * q + r))
        for r in range(4)
    ]
    for args in rel_args:
        push(*args)

    @pl.loop(GROUPS, 2 * GROUPS)
    def _(g):
        group(g, False)

    for args in res_args:
        push(*args)

    con_local.wait()
    pl.when(has_cl)(lambda: to_cr.wait_recv())
    pl.when(has_cr)(lambda: to_cl.wait_recv())

    def chain_fill(layer):
        cond = natural(con_nat, layer)
        for n in range(3):
            kappa = cond * (1.0 / COARSE_ROOTS[n])
            kc[n, layer] = kappa
            mc[n, layer] = 1.0 - 6.0 * kappa

    for layer in range(CH, CH + 4):
        chain_fill(layer)
    for has, first in ((has_cl, 0), (has_cr, CH + 4)):
        @pl.when(has)
        def _(first=first):
            for layer in range(first, first + CH):
                chain_fill(layer)

        @pl.when(jnp.logical_not(has))
        def _(first=first):
            for layer in range(first, first + CH):
                for n in range(3):
                    kc[n, layer] = nothing
                    mc[n, layer] = nothing
                eb[0, layer] = nothing
                eb[1, layer] = nothing

    def out_rows(ref, i, layer, value):
        for j in range(8):
            ref[i, layer, pl.ds(j, 8, stride=8), :] = value[j]

    def chain_copies(i):
        p = i % 2
        core = jnp.where(i == 3, 1, m)
        lft, rgt = (core, c - 1), (core, c + 1)
        return (
            remote(eb.at[p, pl.ds(CH, CH)], eb.at[p, pl.ds(CH + 4, CH)], chain_send.at[0, p], chain_recv.at[0, p], lft),
            remote(eb.at[p, pl.ds(4, CH)], eb.at[p, pl.ds(0, CH)], chain_send.at[1, p], chain_recv.at[1, p], rgt),
        )

    over = remote(eb.at[1, pl.ds(CH, 4)], eb.at[1, pl.ds(CH, 4)], chain_send.at[2, 0], chain_recv.at[2, 0], (1, c))

    @pl.loop(0, 4)
    def _(i):
        p = i % 2
        o = 1 - p
        arrived(res_in.at[i], out_recv.at[1, i])
        start = jnp.logical_and(m == 0, i == 0)

        @pl.when(start)
        def _():
            for layer in range(4):
                eb[p, CH + layer] = res_in[i, layer]

        @pl.when(jnp.logical_not(start))
        def _():
            a, b = chain_copies(i + 1)
            pl.when(has_cr)(lambda: a.wait_recv())
            pl.when(has_cl)(lambda: b.wait_recv())
            pl.when(i == 0)(lambda: over.wait_recv())

            @pl.when(i >= 2)
            def _():
                d, e = chain_copies(i - 2)
                pl.when(has_cl)(lambda: d.wait_send())
                pl.when(has_cr)(lambda: e.wait_send())

            src = eb.at[o]
            for n, dst in enumerate((t1, t2, None)):
                for layer in range(n + 1, CT - n - 1):
                    centre = src[layer]
                    total = neighbours(src[layer - 1], centre, src[layer + 1], mk)
                    value = mc[n, layer] * centre + kc[n, layer] * total
                    if dst is None:
                        eb[p, layer] = value + res_in[i, layer - CH]
                    else:
                        dst[layer] = value
                src = dst

        d, e = chain_copies(i)
        more = jnp.logical_or(i < 3, m == 0)
        pl.when(jnp.logical_and(more, has_cl))(lambda: d.start())
        pl.when(jnp.logical_and(more, has_cr))(lambda: e.start())
        pl.when(jnp.logical_and(i == 3, m == 0))(lambda: over.start())
        arrived(rel_in.at[i], out_recv.at[0, i])
        for layer in range(4):
            out_rows(residual, i, layer, res_in[i, layer])
            out_rows(corrected, i, layer, rel_in[i, layer] + eb[p, CH + layer])

    d, e = chain_copies(2)
    pl.when(has_cl)(lambda: d.wait_send())
    pl.when(has_cr)(lambda: e.wait_send())
    d, e = chain_copies(3)

    @pl.when(m == 0)
    def _():
        pl.when(has_cl)(lambda: d.wait_send())
        pl.when(has_cr)(lambda: e.wait_send())
        over.wait_send()

    for args, when in sends:
        if when is None:
            pushed(*args)
        else:
            pl.when(when)(lambda: pushed(*args))
    pl.when(m == 0)(lambda: pushed(initial, nat.at[1, place], in_send.at[1, 4], in_recv.at[1, sr], device(0, sq)))
    for array in (0, 2):
        for relay in relays[array]:
            relay.wait_send()
    sub.wait_send()
    for to_l, to_r in nat_copies:
        pl.when(has_l)(lambda: to_l.wait_send())
        pl.when(has_r)(lambda: to_r.wait_send())
    pl.when(has_cl)(lambda: to_cl.wait_send())
    pl.when(has_cr)(lambda: to_cr.wait_send())
    to_partner.wait_send()
    for args in rel_args + res_args:
        pushed(*args)
    a, b = state_copies(2 * GROUPS - 1)
    pl.when(has_l)(lambda: a.wait_send())
    pl.when(has_r)(lambda: b.wait_send())


def body(initial, guess, conduct, source, profile):
    amount = jnp.broadcast_to(profile[:, None], (4 * COARSEN, 128))
    anyspace = pl.BlockSpec(memory_space=pl.ANY)
    vmem = pl.BlockSpec(memory_space=pltpu.VMEM)
    out = jax.ShapeDtypeStruct((4, 4, 64, 128), F32)
    dma = pltpu.SemaphoreType.DMA

    def layers(*lead):
        return pltpu.VMEM((*lead, 8, 8, 128), F32)

    return pl.pallas_call(
        kernel,
        name="mgrit",
        out_shape=(out, out),
        in_specs=[anyspace, anyspace, anyspace, anyspace, vmem],
        out_specs=(vmem, vmem),
        scratch_shapes=[
            pltpu.VMEM((4, LT, 64, 128), F32),
            pltpu.VMEM((CT, 64, 128), F32),
            pltpu.VMEM((2, 4 * COARSEN, 128), F32),
            layers(4, LT),
            layers(3, LT),
            layers(LT),
            layers(LT),
            layers(LT),
            layers(2, 2, H),
            layers(2, 2, H),
            layers(B),
            layers(3, CT),
            layers(3, CT),
            layers(2, CT),
            layers(CT),
            layers(CT),
            layers(4, 4),
            layers(4, 4),
            dma((4, 5)), dma((4, 4)),
            dma((2, 3)), dma((2, 3)),
            dma((2,)), dma((5,)), dma((2,)),
            dma((2, 2)), dma((2, 2)),
            dma((2, 4)), dma((2, 4)),
            dma((3, 2)), dma((3, 2)),
        ],
        compiler_params=pltpu.CompilerParams(
            has_side_effects=True, vmem_limit_bytes=67043328
        ),
    )(initial, guess, conduct, source, amount)


def solution(mesh):
    return jax.shard_map(
        body,
        mesh=mesh,
        in_specs=(
            P("space", None, None),
            P("tm", "space", None, None),
            P("space", None, None),
            P("space", None, None),
            P("tm"),
        ),
        out_specs=(P("tm", "space", None, None), P("tm", "space", None, None)),
        check_vma=False,
    )
```

```python
import numpy as np
import jax
import jax.numpy as jnp
from jax import lax
from jax.experimental import pallas as pl
from jax.experimental.pallas import tpu as pltpu
from jax.sharding import PartitionSpec as P

SWEEPS = 3
KAPPA_TOP = 3.0
COARSEN = 8
H = 6
B = 16
LT = B + 2 * H
GROUPS = COARSEN * SWEEPS // H
CH = 3
CT = 4 + 2 * CH
F32 = jnp.float32
MESH = pl.DeviceIdType.MESH


def polynomials(scale, top):
    middle, spread = (top + 1.0) / 2.0, (top - 1.0) / 2.0
    relative = middle / spread
    ratio = 1.0 / relative
    one = np.polynomial.Polynomial([1.0])
    system = np.polynomial.Polynomial([1.0, scale])
    remain = one
    update = remain / middle
    total = update
    for _ in range(SWEEPS - 1):
        remain = remain - system * update
        following = 1.0 / (2.0 * relative - ratio)
        update = following * ratio * update + 2.0 * following / spread * remain
        total = total + update
        ratio = following
    rest = one - np.polynomial.Polynomial([0.0, scale]) * total
    return [float(r) for r in np.sort(rest.roots().real)], [float(c) for c in total.coef]


FINE_ROOTS, FINE_P = polynomials(1.0, 1.0 + 12.0 * KAPPA_TOP)
COARSE_ROOTS, _ = polynomials(float(COARSEN), 1.0 + 12.0 * KAPPA_TOP * COARSEN)


class Masks:
    def __init__(self):
        lane = lax.broadcasted_iota(jnp.int32, (8, 8, 128), 2)
        sub = lax.broadcasted_iota(jnp.int32, (8, 128), 0)
        self.first_lane, self.last_lane = lane == 0, lane == 127
        self.first_sub, self.last_sub = sub == 0, sub == 7


def neighbours(below, centre, above, mk):
    side = jnp.where(mk.first_lane, 0.0, pltpu.roll(centre, 1, 2))
    side = side + jnp.where(mk.last_lane, 0.0, pltpu.roll(centre, 127, 2))
    before = jnp.where(mk.first_sub, 0.0, pltpu.roll(centre[7], 1, 0))
    after = jnp.where(mk.last_sub, 0.0, pltpu.roll(centre[0], 7, 0))
    rows = jnp.concatenate([before[None], centre[:7]], axis=0) + jnp.concatenate(
        [centre[1:], after[None]], axis=0
    )
    return (side + rows) + (below + above)


def natural(ref, layer):
    return jnp.stack([ref[layer, pl.ds(j, 8, stride=8), :] for j in range(8)], axis=0)


def kernel(
    initial, guess, conduct, source, amount,
    corrected, residual,
    nat, con_nat, prof, kap, mul, grow, ua, ub, land, stage, rel, kc, mc, eb, t1, t2, res_in, rel_in,
    in_send, in_recv, nat_send, nat_recv, prof_sem, con_sem, sub_sem, halo_send, halo_recv,
    out_send, out_recv, chain_send, chain_recv,
):
    m = lax.axis_index("tm")
    c = lax.axis_index("space")
    mk = Masks()

    x, y, z = c % 4, (c // 4) % 4, c // 16
    half = y // 2
    s = jnp.where(half == 0, y, 3 - y)
    k = x + 4 * half
    q = 2 * (2 * z + (s + z) % 2) + m

    def device(kk, qq):
        b = qq // 2
        zz = b // 2
        ss = (b % 2 + zz % 2) % 2
        yy = jnp.where(kk // 4 == 0, ss, 3 - ss)
        return (qq % 2, zz * 16 + yy * 4 + kk % 4)

    def remote(src, dst, ssem, rsem, to):
        return pltpu.make_async_remote_copy(
            src_ref=src, dst_ref=dst, send_sem=ssem, recv_sem=rsem, device_id=to, device_id_type=MESH
        )

    def is_me(to):
        return jnp.logical_and(to[0] == m, to[1] == c)

    def push(src, dst, ssem, rsem, to):
        mine = is_me(to)

        @pl.when(mine)
        def _():
            pltpu.make_async_copy(src, dst, rsem).start()

        @pl.when(jnp.logical_not(mine))
        def _():
            remote(src, dst, ssem, rsem, to).start()

    def pushed(src, dst, ssem, rsem, to):
        @pl.when(jnp.logical_not(is_me(to)))
        def _():
            remote(src, dst, ssem, rsem, to).wait_send()

    def arrived(dst, rsem):
        pltpu.make_async_copy(dst, dst, rsem).wait()

    left, right = device(k, jnp.maximum(q - 1, 0)), device(k, jnp.minimum(q + 1, 15))
    has_l, has_r = q > 0, q < 15
    sq, sr = c // 4, c % 4
    has_cl, has_cr = c > 0, c < 63
    barrier = pltpu.get_barrier_semaphore()

    def hello(to):
        pl.semaphore_signal(barrier, inc=1, device_id=to, device_id_type=MESH)

    for kk in range(8):
        for to in (device(kk, sq), (kk // 4, 4 * q + kk % 4)):
            pl.when(jnp.logical_not(is_me(to)))(lambda: hello(to))
    for d in range(1, 8):
        hello(device((k + d) % 8, q))
    hello((1 - m, c))
    hello(device(k, (q + 1) % 16))
    hello(device(k, (q + 15) % 16))
    for d in (1, 63):
        hello((0, (c + d) % 64))
        hello((1, (c + d) % 64))
    pl.semaphore_wait(barrier, 30 - 2 * jnp.where(sq == q, 1, 0))

    place = pl.ds(H + 4 * sr, 4)
    own = pl.ds(H, B)
    sends = []

    def give(array, slot, src, kk, when=None):
        args = (src, nat.at[array, place], in_send.at[array, slot], in_recv.at[array, sr], device(kk, sq))
        sends.append((args, when))
        if when is None:
            push(*args)
        else:
            pl.when(when)(lambda: push(*args))

    chain_left, chain_right = (m, c - 1), (m, c + 1)
    con_local = pltpu.make_async_copy(conduct, con_nat.at[pl.ds(CH, 4)], con_sem.at[0])
    to_cl = remote(conduct.at[pl.ds(0, CH)], con_nat.at[pl.ds(CH + 4, CH)], con_sem.at[1], con_sem.at[2], chain_left)
    to_cr = remote(conduct.at[pl.ds(1, CH)], con_nat.at[pl.ds(0, CH)], con_sem.at[3], con_sem.at[4], chain_right)

    partner = (1 - m, c)
    to_partner = remote(amount, prof.at[m], prof_sem.at[0], prof_sem.at[1], partner)

    give(0, 0, conduct, x + 4 * m)
    give(2, 0, source, x + 4 * m)
    relays = {}
    for array in (0, 2):
        column = nat.at[array, pl.ds(H + 4 * x, 4)]
        relays[array] = [
            remote(column, column, in_send.at[array, d], in_recv.at[array, x], (m, 16 * z + 4 * y + (x + d) % 4)) for d in range(1, 4)
        ]
        arrived(column, in_recv.at[array, x])
        for relay in relays[array]:
            relay.start()
    pl.when(m == 0)(lambda: push(initial, nat.at[1, place], in_send.at[1, 4], in_recv.at[1, sr], device(0, sq)))
    for i in range(3):
        give(1, i, guess.at[i], 4 * m + i + 1)
    give(1, 3, guess.at[3], 4, m == 0)
    prof[m] = amount[...]

    nat_copies = []

    def beside(array):
        to_l = remote(
            nat.at[array, pl.ds(H, H)], nat.at[array, pl.ds(H + B, H)],
            nat_send.at[0, array], nat_recv.at[0, array], left,
        )
        to_r = remote(
            nat.at[array, pl.ds(B, H)], nat.at[array, pl.ds(0, H)],
            nat_send.at[1, array], nat_recv.at[1, array], right,
        )
        nat_copies.append((to_l, to_r))

        def piece(r):
            def come():
                arrived(nat.at[array, pl.ds(H + 4 * r, 4)], in_recv.at[array, r])

            if array == 1:
                come()
            else:
                pl.when(x != r)(come)

        piece(0)
        piece(1)
        pl.when(has_l)(lambda: to_l.start())
        piece(2)
        piece(3)
        pl.when(has_r)(lambda: to_r.start())

    def halo_arrived(array):
        pl.when(has_r)(lambda: arrived(nat.at[array, pl.ds(H + B, H)], nat_recv.at[0, array]))
        pl.when(has_l)(lambda: arrived(nat.at[array, pl.ds(0, H)], nat_recv.at[1, array]))

    def coefficients(layer, cond):
        for n in range(3):
            kappa = cond * (1.0 / FINE_ROOTS[n])
            kap[n, layer] = kappa
            mul[n, layer] = 1.0 - 6.0 * kappa
        kap[3, layer] = cond

    nothing = jnp.zeros((8, 8, 128), F32)

    def edges(has, first, fill, blank):
        @pl.when(has)
        def _():
            @pl.loop(first, first + H)
            def _(layer):
                fill(layer)

        @pl.when(jnp.logical_not(has))
        def _():
            @pl.loop(first, first + H)
            def _(layer):
                blank(layer)

    def fill_con(layer):
        coefficients(layer, natural(nat.at[0], layer))

    def blank_con(layer):
        for n in range(3):
            kap[n, layer] = nothing
            mul[n, layer] = nothing
        kap[3, layer] = nothing

    def fill_src(layer):
        ub[layer] = natural(nat.at[2], layer)

    def blank_src(layer):
        ub[layer] = nothing

    beside(0)

    @pl.loop(H, H + B)
    def _(layer):
        fill_con(layer)

    beside(2)
    halo_arrived(0)
    edges(has_l, 0, fill_con, blank_con)
    edges(has_r, H + B, fill_con, blank_con)

    @pl.loop(H, H + B)
    def _(layer):
        fill_src(layer)

    halo_arrived(2)
    edges(has_l, 0, fill_src, blank_src)
    edges(has_r, H + B, fill_src, blank_src)

    def applied(ref, layer):
        centre = ref[layer]
        return kap[3, layer] * (6.0 * centre - neighbours(ref[layer - 1], centre, ref[layer + 1], mk))

    @pl.loop(1, LT - 1)
    def _(layer):
        ua[layer] = FINE_P[1] * ub[layer] + FINE_P[2] * applied(ub, layer)

    @pl.loop(2, LT - 2)
    def _(layer):
        grow[layer] = FINE_P[0] * ub[layer] + applied(ua, layer)

    beside(1)
    sub_src, sub_dst = nat.at[1, own], nat.at[3, own]
    sub = remote(sub_src, sub_dst, sub_sem.at[0], sub_sem.at[1], device((k + 7) % 8, q))
    sub.start()
    con_local.start()
    to_partner.start()
    pl.when(has_cl)(lambda: to_cl.start())
    pl.when(has_cr)(lambda: to_cr.start())

    @pl.loop(H, H + B)
    def _(layer):
        ua[layer] = natural(nat.at[1], layer)

    halo_arrived(1)
    for side, has, first in ((0, has_l, 0), (1, has_r, H + B)):
        def fill(layer, side=side, first=first):
            land[0, side, layer - first] = natural(nat.at[1], layer)

        def blank(layer, side=side, first=first):
            land[0, side, layer - first] = nothing
            land[1, side, layer - first] = nothing

        edges(has, first, fill, blank)

    arrived(prof.at[1 - m], prof_sem.at[1])

    def state_copies(t):
        p = t % 2
        return (
            remote(stage.at[p, 0], land.at[p, 1], halo_send.at[0, p], halo_recv.at[0, p], left),
            remote(stage.at[p, 1], land.at[p, 0], halo_send.at[1, p], halo_recv.at[1, p], right),
        )

    def group(g, with_source):
        parity = g % 2
        following = (g + 1) % 2
        bufs = (ua, ub)

        def read(i, layer):
            if i == 0 and layer < H:
                return land[parity, 0, layer]
            if i == 0 and layer >= H + B:
                return land[parity, 1, layer - H - B]
            return bufs[i % 2][layer]

        amounts = {}
        if with_source:
            for n in range(H // 3):
                row = prof[k // 4, pl.ds(COARSEN * (k % 4) + g * (H // 3) + n, 1), :]
                amounts[3 * n + 3] = jnp.broadcast_to(row, (8, 128))

        def region(bounds, sent=None):
            todo = []
            for i in range(1, H + 1):
                lo, hi = bounds(i)
                todo += [(layer + 2 * i, i, layer) for layer in range(lo, hi)]
            for _, i, layer in sorted(todo):
                n = (i - 1) % 3
                centre = read(i - 1, layer)
                total = neighbours(read(i - 1, layer - 1), centre, read(i - 1, layer + 1), mk)
                value = mul[n, layer] * centre + kap[n, layer] * total
                if i in amounts:
                    value = value + amounts[i][None] * grow[layer]
                bufs[i % 2][layer] = value
                if i == H and sent is not None:
                    stage[following, sent[0], layer - sent[1]] = value

        @pl.when(g >= 2)
        def _():
            a, b = state_copies(g + 1)
            pl.when(has_l)(lambda: a.wait_send())
            pl.when(has_r)(lambda: b.wait_send())

        region(lambda i: (H + i, H + B - i))
        a, b = state_copies(g)
        c_, d_ = state_copies(g + 1)
        last = COARSEN * SWEEPS // H

        @pl.when(jnp.logical_and(g > 0, has_l))
        def _():
            b.wait_recv()

        region(lambda i: (i, H + i), (0, H))

        @pl.when(jnp.logical_and((g + 1) % last != 0, has_l))
        def _():
            c_.start()

        @pl.when(jnp.logical_and(g > 0, has_r))
        def _():
            a.wait_recv()

        region(lambda i: (LT - H - i, LT - i), (1, B))

        @pl.when(jnp.logical_and((g + 1) % last != 0, has_r))
        def _():
            d_.start()

    @pl.loop(0, GROUPS)
    def _(g):
        group(g, True)

    arrived(sub_dst, sub_sem.at[1])
    first_copies = state_copies(GROUPS)
    final = k == 7

    def difference(layer):
        value = ua[layer]
        off = natural(nat.at[3], layer)
        rel[layer - H] = value
        value = jnp.where(final, off, value) - off
        ua[layer] = value
        return value

    @pl.loop(0, H)
    def _(i):
        stage[GROUPS % 2, 0, i] = difference(H + i)

    pl.when(has_l)(lambda: first_copies[0].start())

    @pl.loop(2 * H, B)
    def _(layer):
        difference(layer)

    @pl.loop(0, H)
    def _(i):
        stage[GROUPS % 2, 1, i] = difference(B + i)

    pl.when(has_r)(lambda: first_copies[1].start())

    after = (k + 1) % 8
    rel_args = [
        (rel.at[pl.ds(4 * r, 4)], rel_in.at[k % 4], out_send.at[0, r], out_recv.at[0, k % 4], (k // 4, 4 * q + r))
        for r in range(4)
    ]
    res_args = [
        (ua.at[pl.ds(H + 4 * r, 4)], res_in.at[after % 4], out_send.at[1, r], out_recv.at[1, after % 4], (after // 4, 4 * q + r))
        for r in range(4)
    ]
    for args in rel_args:
        push(*args)

    @pl.loop(GROUPS, 2 * GROUPS)
    def _(g):
        group(g, False)

    for args in res_args:
        push(*args)

    con_local.wait()
    pl.when(has_cl)(lambda: to_cr.wait_recv())
    pl.when(has_cr)(lambda: to_cl.wait_recv())

    def chain_fill(layer):
        cond = natural(con_nat, layer)
        for n in range(3):
            kappa = cond * (1.0 / COARSE_ROOTS[n])
            kc[n, layer] = kappa
            mc[n, layer] = 1.0 - 6.0 * kappa

    for layer in range(CH, CH + 4):
        chain_fill(layer)
    for has, first in ((has_cl, 0), (has_cr, CH + 4)):
        @pl.when(has)
        def _(first=first):
            for layer in range(first, first + CH):
                chain_fill(layer)

        @pl.when(jnp.logical_not(has))
        def _(first=first):
            for layer in range(first, first + CH):
                for n in range(3):
                    kc[n, layer] = nothing
                    mc[n, layer] = nothing
                eb[0, layer] = nothing
                eb[1, layer] = nothing

    def out_rows(ref, i, layer, value):
        for j in range(8):
            ref[i, layer, pl.ds(j, 8, stride=8), :] = value[j]

    def chain_copies(i):
        p = i % 2
        core = jnp.where(i == 3, 1, m)
        lft, rgt = (core, c - 1), (core, c + 1)
        return (
            remote(eb.at[p, pl.ds(CH, CH)], eb.at[p, pl.ds(CH + 4, CH)], chain_send.at[0, p], chain_recv.at[0, p], lft),
            remote(eb.at[p, pl.ds(4, CH)], eb.at[p, pl.ds(0, CH)], chain_send.at[1, p], chain_recv.at[1, p], rgt),
        )

    over = remote(eb.at[1, pl.ds(CH, 4)], eb.at[1, pl.ds(CH, 4)], chain_send.at[2, 0], chain_recv.at[2, 0], (1, c))

    @pl.loop(0, 4)
    def _(i):
        p = i % 2
        o = 1 - p
        arrived(res_in.at[i], out_recv.at[1, i])
        start = jnp.logical_and(m == 0, i == 0)

        @pl.when(start)
        def _():
            for layer in range(4):
                eb[p, CH + layer] = res_in[i, layer]

        @pl.when(jnp.logical_not(start))
        def _():
            a, b = chain_copies(i + 1)
            pl.when(has_cr)(lambda: a.wait_recv())
            pl.when(has_cl)(lambda: b.wait_recv())
            pl.when(i == 0)(lambda: over.wait_recv())

            @pl.when(i >= 2)
            def _():
                d, e = chain_copies(i - 2)
                pl.when(has_cl)(lambda: d.wait_send())
                pl.when(has_cr)(lambda: e.wait_send())

            src = eb.at[o]
            for n, dst in enumerate((t1, t2, None)):
                for layer in range(n + 1, CT - n - 1):
                    centre = src[layer]
                    total = neighbours(src[layer - 1], centre, src[layer + 1], mk)
                    value = mc[n, layer] * centre + kc[n, layer] * total
                    if dst is None:
                        eb[p, layer] = value + res_in[i, layer - CH]
                    else:
                        dst[layer] = value
                src = dst

        d, e = chain_copies(i)
        more = jnp.logical_or(i < 3, m == 0)
        pl.when(jnp.logical_and(more, has_cl))(lambda: d.start())
        pl.when(jnp.logical_and(more, has_cr))(lambda: e.start())
        pl.when(jnp.logical_and(i == 3, m == 0))(lambda: over.start())
        arrived(rel_in.at[i], out_recv.at[0, i])
        for layer in range(4):
            out_rows(residual, i, layer, res_in[i, layer])
            out_rows(corrected, i, layer, rel_in[i, layer] + eb[p, CH + layer])

    d, e = chain_copies(2)
    pl.when(has_cl)(lambda: d.wait_send())
    pl.when(has_cr)(lambda: e.wait_send())
    d, e = chain_copies(3)

    @pl.when(m == 0)
    def _():
        pl.when(has_cl)(lambda: d.wait_send())
        pl.when(has_cr)(lambda: e.wait_send())
        over.wait_send()

    for args, when in sends:
        if when is None:
            pushed(*args)
        else:
            pl.when(when)(lambda: pushed(*args))
    pl.when(m == 0)(lambda: pushed(initial, nat.at[1, place], in_send.at[1, 4], in_recv.at[1, sr], device(0, sq)))
    for array in (0, 2):
        for relay in relays[array]:
            relay.wait_send()
    sub.wait_send()
    for to_l, to_r in nat_copies:
        pl.when(has_l)(lambda: to_l.wait_send())
        pl.when(has_r)(lambda: to_r.wait_send())
    pl.when(has_cl)(lambda: to_cl.wait_send())
    pl.when(has_cr)(lambda: to_cr.wait_send())
    to_partner.wait_send()
    for args in rel_args + res_args:
        pushed(*args)
    a, b = state_copies(2 * GROUPS - 1)
    pl.when(has_l)(lambda: a.wait_send())
    pl.when(has_r)(lambda: b.wait_send())


def body(initial, guess, conduct, source, profile):
    amount = jnp.broadcast_to(profile[:, None], (4 * COARSEN, 128))
    anyspace = pl.BlockSpec(memory_space=pl.ANY)
    vmem = pl.BlockSpec(memory_space=pltpu.VMEM)
    out = jax.ShapeDtypeStruct((4, 4, 64, 128), F32)
    dma = pltpu.SemaphoreType.DMA

    def layers(*lead):
        return pltpu.VMEM((*lead, 8, 8, 128), F32)

    return pl.pallas_call(
        kernel,
        name="mgrit",
        out_shape=(out, out),
        in_specs=[anyspace, anyspace, anyspace, anyspace, vmem],
        out_specs=(vmem, vmem),
        scratch_shapes=[
            pltpu.VMEM((4, LT, 64, 128), F32),
            pltpu.VMEM((CT, 64, 128), F32),
            pltpu.VMEM((2, 4 * COARSEN, 128), F32),
            layers(4, LT),
            layers(3, LT),
            layers(LT),
            layers(LT),
            layers(LT),
            layers(2, 2, H),
            layers(2, 2, H),
            layers(B),
            layers(3, CT),
            layers(3, CT),
            layers(2, CT),
            layers(CT),
            layers(CT),
            layers(4, 4),
            layers(4, 4),
            dma((4, 5)), dma((4, 4)),
            dma((2, 3)), dma((2, 3)),
            dma((2,)), dma((5,)), dma((2,)),
            dma((2, 2)), dma((2, 2)),
            dma((2, 4)), dma((2, 4)),
            dma((3, 2)), dma((3, 2)),
        ],
        compiler_params=pltpu.CompilerParams(
            collective_id=0, has_side_effects=True, vmem_limit_bytes=67043328
        ),
    )(initial, guess, conduct, source, amount)


def solution(mesh):
    return jax.shard_map(
        body,
        mesh=mesh,
        in_specs=(
            P("space", None, None),
            P("tm", "space", None, None),
            P("space", None, None),
            P("space", None, None),
            P("tm"),
        ),
        out_specs=(P("tm", "space", None, None), P("tm", "space", None, None)),
        check_vma=False,
    )
```

```python
import numpy as np
import jax
import jax.numpy as jnp
from jax import lax
from jax.experimental import pallas as pl
from jax.experimental.pallas import tpu as pltpu
from jax.sharding import PartitionSpec as P

SWEEPS = 3
KAPPA_TOP = 3.0
COARSEN = 8
H = 6
B = 16
LT = B + 2 * H
GROUPS = COARSEN * SWEEPS // H
CH = 3
CT = 4 + 2 * CH
F32 = jnp.float32
MESH = pl.DeviceIdType.MESH


def polynomials(scale, top):
    middle, spread = (top + 1.0) / 2.0, (top - 1.0) / 2.0
    relative = middle / spread
    ratio = 1.0 / relative
    one = np.polynomial.Polynomial([1.0])
    system = np.polynomial.Polynomial([1.0, scale])
    remain = one
    update = remain / middle
    total = update
    for _ in range(SWEEPS - 1):
        remain = remain - system * update
        following = 1.0 / (2.0 * relative - ratio)
        update = following * ratio * update + 2.0 * following / spread * remain
        total = total + update
        ratio = following
    rest = one - np.polynomial.Polynomial([0.0, scale]) * total
    return [float(r) for r in np.sort(rest.roots().real)], [float(c) for c in total.coef]


FINE_ROOTS, FINE_P = polynomials(1.0, 1.0 + 12.0 * KAPPA_TOP)
COARSE_ROOTS, _ = polynomials(float(COARSEN), 1.0 + 12.0 * KAPPA_TOP * COARSEN)


class Masks:
    def __init__(self):
        lane = lax.broadcasted_iota(jnp.int32, (8, 8, 128), 2)
        sub = lax.broadcasted_iota(jnp.int32, (8, 128), 0)
        self.first_lane, self.last_lane = lane == 0, lane == 127
        self.first_sub, self.last_sub = sub == 0, sub == 7


def neighbours(below, centre, above, mk):
    side = jnp.where(mk.first_lane, 0.0, pltpu.roll(centre, 1, 2))
    side = side + jnp.where(mk.last_lane, 0.0, pltpu.roll(centre, 127, 2))
    before = jnp.where(mk.first_sub, 0.0, pltpu.roll(centre[7], 1, 0))
    after = jnp.where(mk.last_sub, 0.0, pltpu.roll(centre[0], 7, 0))
    rows = jnp.concatenate([before[None], centre[:7]], axis=0) + jnp.concatenate(
        [centre[1:], after[None]], axis=0
    )
    return (side + rows) + (below + above)


def natural(ref, layer):
    return jnp.stack([ref[layer, pl.ds(j, 8, stride=8), :] for j in range(8)], axis=0)


def each(lo, hi, run, unroll):
    assert (hi - lo) % unroll == 0

    @pl.loop(0, (hi - lo) // unroll)
    def _(t):
        for d in range(unroll):
            run(lo + t * unroll + d)


def kernel(
    initial, guess, conduct, source, amount,
    corrected, residual,
    nat, con_nat, prof, kap, mul, grow, ua, ub, land, stage, rel, kc, mc, eb, t1, t2, res_in, rel_in,
    in_send, in_recv, nat_send, nat_recv, prof_sem, con_sem, sub_sem, halo_send, halo_recv,
    out_send, out_recv, chain_send, chain_recv, turn,
):
    m = lax.axis_index("tm")
    c = lax.axis_index("space")
    mk = Masks()

    x, y, z = c % 4, (c // 4) % 4, c // 16
    half = y // 2
    s = jnp.where(half == 0, y, 3 - y)
    k = x + 4 * half
    q = 2 * (2 * z + (s + z) % 2) + m

    def device(kk, qq):
        b = qq // 2
        zz = b // 2
        ss = (b % 2 + zz % 2) % 2
        yy = jnp.where(kk // 4 == 0, ss, 3 - ss)
        return (qq % 2, zz * 16 + yy * 4 + kk % 4)

    def remote(src, dst, ssem, rsem, to):
        return pltpu.make_async_remote_copy(
            src_ref=src, dst_ref=dst, send_sem=ssem, recv_sem=rsem, device_id=to, device_id_type=MESH
        )

    def is_me(to):
        return jnp.logical_and(to[0] == m, to[1] == c)

    def push(src, dst, ssem, rsem, to):
        mine = is_me(to)

        @pl.when(mine)
        def _():
            pltpu.make_async_copy(src, dst, rsem).start()

        @pl.when(jnp.logical_not(mine))
        def _():
            remote(src, dst, ssem, rsem, to).start()

    def pushed(src, dst, ssem, rsem, to):
        @pl.when(jnp.logical_not(is_me(to)))
        def _():
            remote(src, dst, ssem, rsem, to).wait_send()

    def arrived(dst, rsem):
        pltpu.make_async_copy(dst, dst, rsem).wait()

    left, right = device(k, jnp.maximum(q - 1, 0)), device(k, jnp.minimum(q + 1, 15))
    has_l, has_r = q > 0, q < 15
    sq, sr = c // 4, c % 4
    has_cl, has_cr = c > 0, c < 63
    barrier = pltpu.get_barrier_semaphore()

    def hello(to):
        pl.semaphore_signal(barrier, inc=1, device_id=to, device_id_type=MESH)

    for kk in range(8):
        for to in (device(kk, sq), (kk // 4, 4 * q + kk % 4)):
            pl.when(jnp.logical_not(is_me(to)))(lambda: hello(to))
    for d in range(1, 8):
        hello(device((k + d) % 8, q))
    hello((1 - m, c))
    hello(device(k, (q + 1) % 16))
    hello(device(k, (q + 15) % 16))
    for d in (1, 63):
        hello((0, (c + d) % 64))
        hello((1, (c + d) % 64))
    pl.semaphore_wait(barrier, 30 - 2 * jnp.where(sq == q, 1, 0))

    place = pl.ds(H + 4 * sr, 4)
    own = pl.ds(H, B)
    sends = []

    def give(array, slot, src, kk, when=None):
        args = (src, nat.at[array, place], in_send.at[array, slot], in_recv.at[array, sr], device(kk, sq))
        sends.append((args, when))
        if when is None:
            push(*args)
        else:
            pl.when(when)(lambda: push(*args))

    chain_left, chain_right = (m, c - 1), (m, c + 1)
    con_local = pltpu.make_async_copy(conduct, con_nat.at[pl.ds(CH, 4)], con_sem.at[0])
    to_cl = remote(conduct.at[pl.ds(0, CH)], con_nat.at[pl.ds(CH + 4, CH)], con_sem.at[1], con_sem.at[2], chain_left)
    to_cr = remote(conduct.at[pl.ds(1, CH)], con_nat.at[pl.ds(0, CH)], con_sem.at[3], con_sem.at[4], chain_right)

    partner = (1 - m, c)
    to_partner = remote(amount, prof.at[m], prof_sem.at[0], prof_sem.at[1], partner)

    give(0, 0, conduct, x + 4 * m)
    give(2, 0, source, x + 4 * m)
    relays = {}
    for array in (0, 2):
        column = nat.at[array, pl.ds(H + 4 * x, 4)]
        relays[array] = [
            remote(column, column, in_send.at[array, d], in_recv.at[array, x], (m, 16 * z + 4 * y + (x + d) % 4)) for d in range(1, 4)
        ]
        arrived(column, in_recv.at[array, x])
        for relay in relays[array]:
            relay.start()
    pl.when(m == 0)(lambda: push(initial, nat.at[1, place], in_send.at[1, 4], in_recv.at[1, sr], device(0, sq)))
    for i in range(3):
        give(1, i, guess.at[i], 4 * m + i + 1)
    give(1, 3, guess.at[3], 4, m == 0)
    prof[m] = amount[...]

    nat_copies = []

    def beside(array):
        to_l = remote(
            nat.at[array, pl.ds(H, H)], nat.at[array, pl.ds(H + B, H)],
            nat_send.at[0, array], nat_recv.at[0, array], left,
        )
        to_r = remote(
            nat.at[array, pl.ds(B, H)], nat.at[array, pl.ds(0, H)],
            nat_send.at[1, array], nat_recv.at[1, array], right,
        )
        nat_copies.append((to_l, to_r))

        def piece(r):
            def come():
                arrived(nat.at[array, pl.ds(H + 4 * r, 4)], in_recv.at[array, r])

            if array == 1:
                come()
            else:
                pl.when(x != r)(come)

        piece(0)
        piece(1)
        pl.when(has_l)(lambda: to_l.start())
        piece(2)
        piece(3)
        pl.when(has_r)(lambda: to_r.start())

    def halo_arrived(array):
        pl.when(has_r)(lambda: arrived(nat.at[array, pl.ds(H + B, H)], nat_recv.at[0, array]))
        pl.when(has_l)(lambda: arrived(nat.at[array, pl.ds(0, H)], nat_recv.at[1, array]))

    def coefficients(layer, cond):
        for n in range(3):
            kappa = cond * (1.0 / FINE_ROOTS[n])
            kap[n, layer] = kappa
            mul[n, layer] = 1.0 - 6.0 * kappa
        kap[3, layer] = cond

    nothing = jnp.zeros((8, 8, 128), F32)

    def edges(has, first, fill, blank):
        @pl.when(has)
        def _():
            each(first, first + H, fill, 3)

        @pl.when(jnp.logical_not(has))
        def _():
            each(first, first + H, blank, 3)

    def fill_con(layer):
        coefficients(layer, natural(nat.at[0], layer))

    def blank_con(layer):
        for n in range(3):
            kap[n, layer] = nothing
            mul[n, layer] = nothing
        kap[3, layer] = nothing

    def fill_src(layer):
        ub[layer] = natural(nat.at[2], layer)

    def blank_src(layer):
        ub[layer] = nothing

    beside(0)

    each(H, H + B, fill_con, 4)

    beside(2)
    beside(1)
    sub_src, sub_dst = nat.at[1, own], nat.at[3, own]
    sub = remote(sub_src, sub_dst, sub_sem.at[0], sub_sem.at[1], device((k + 7) % 8, q))
    sub.start()
    con_local.start()
    to_partner.start()
    pl.when(has_cl)(lambda: to_cl.start())
    pl.when(has_cr)(lambda: to_cr.start())

    halo_arrived(0)
    edges(has_l, 0, fill_con, blank_con)
    edges(has_r, H + B, fill_con, blank_con)

    each(H, H + B, fill_src, 4)

    halo_arrived(2)
    edges(has_l, 0, fill_src, blank_src)
    edges(has_r, H + B, fill_src, blank_src)

    def applied(ref, layer):
        centre = ref[layer]
        return kap[3, layer] * (6.0 * centre - neighbours(ref[layer - 1], centre, ref[layer + 1], mk))

    def first_power(layer):
        ua[layer] = FINE_P[1] * ub[layer] + FINE_P[2] * applied(ub, layer)

    def second_power(layer):
        grow[layer] = FINE_P[0] * ub[layer] + applied(ua, layer)

    each(1, LT - 1, first_power, (LT - 2) // 2)
    each(2, LT - 2, second_power, (LT - 4) // 2)

    def fill_entry(layer):
        ua[layer] = natural(nat.at[1], layer)

    each(H, H + B, fill_entry, 4)

    def entry_halo(side, has, first, sem):
        def fill(layer):
            land[0, side, layer - first] = natural(nat.at[1], layer)

        def blank(layer):
            land[0, side, layer - first] = nothing
            land[1, side, layer - first] = nothing

        pl.when(has)(lambda: arrived(nat.at[1, pl.ds(first, H)], sem))
        edges(has, first, fill, blank)

    arrived(prof.at[1 - m], prof_sem.at[1])

    def state_copies(t):
        p = t % 2
        return (
            remote(stage.at[p, 0], land.at[p, 1], halo_send.at[0, p], halo_recv.at[0, p], left),
            remote(stage.at[p, 1], land.at[p, 0], halo_send.at[1, p], halo_recv.at[1, p], right),
        )

    def group(g, with_source):
        parity = g % 2
        following = (g + 1) % 2
        bufs = (ua, ub)

        def read(i, layer):
            if i == 0 and layer < H:
                return land[parity, 0, layer]
            if i == 0 and layer >= H + B:
                return land[parity, 1, layer - H - B]
            return bufs[i % 2][layer]

        amounts = {}
        if with_source:
            for n in range(H // 3):
                row = prof[k // 4, pl.ds(COARSEN * (k % 4) + g * (H // 3) + n, 1), :]
                amounts[3 * n + 3] = jnp.broadcast_to(row, (8, 128))

        def region(bounds, sent=None):
            todo = []
            for i in range(1, H + 1):
                lo, hi = bounds(i)
                todo += [(layer + 2 * i, i, layer) for layer in range(lo, hi)]
            for _, i, layer in sorted(todo):
                n = (i - 1) % 3
                centre = read(i - 1, layer)
                total = neighbours(read(i - 1, layer - 1), centre, read(i - 1, layer + 1), mk)
                value = mul[n, layer] * centre + kap[n, layer] * total
                if i in amounts:
                    value = value + amounts[i][None] * grow[layer]
                bufs[i % 2][layer] = value
                if i == H and sent is not None:
                    stage[following, sent[0], layer - sent[1]] = value

        @pl.when(g >= 2)
        def _():
            a, b = state_copies(g + 1)
            pl.when(has_l)(lambda: a.wait_send())
            pl.when(has_r)(lambda: b.wait_send())

        region(lambda i: (H + i, H + B - i))
        a, b = state_copies(g)
        c_, d_ = state_copies(g + 1)
        last = COARSEN * SWEEPS // H

        if with_source:
            pl.when(g == 0)(lambda: entry_halo(0, has_l, 0, nat_recv.at[1, 1]))

        @pl.when(jnp.logical_and(g > 0, has_l))
        def _():
            b.wait_recv()

        region(lambda i: (i, H + i), (0, H))

        @pl.when(jnp.logical_and((g + 1) % last != 0, has_l))
        def _():
            c_.start()

        if with_source:
            pl.when(g == 0)(lambda: entry_halo(1, has_r, H + B, nat_recv.at[0, 1]))

        @pl.when(jnp.logical_and(g > 0, has_r))
        def _():
            a.wait_recv()

        region(lambda i: (LT - H - i, LT - i), (1, B))

        @pl.when(jnp.logical_and((g + 1) % last != 0, has_r))
        def _():
            d_.start()

    @pl.loop(0, GROUPS)
    def _(g):
        group(g, True)

    arrived(sub_dst, sub_sem.at[1])
    first_copies = state_copies(GROUPS)
    final = k == 7

    def difference(layer):
        value = ua[layer]
        off = natural(nat.at[3], layer)
        rel[layer - H] = value
        value = jnp.where(final, off, value) - off
        ua[layer] = value
        return value

    def difference_l(i):
        stage[GROUPS % 2, 0, i] = difference(H + i)

    each(0, H, difference_l, 3)

    pl.when(has_l)(lambda: first_copies[0].start())

    def difference_r(i):
        stage[GROUPS % 2, 1, i] = difference(B + i)

    each(0, H, difference_r, 3)
    pl.when(has_r)(lambda: first_copies[1].start())
    each(2 * H, B, difference, B - 2 * H)

    after = (k + 1) % 8
    rel_args = [
        (rel.at[pl.ds(4 * r, 4)], rel_in.at[k % 4], out_send.at[0, r], out_recv.at[0, k % 4], (k // 4, 4 * q + r))
        for r in range(4)
    ]
    res_args = [
        (ua.at[pl.ds(H + 4 * r, 4)], res_in.at[after % 4], out_send.at[1, r], out_recv.at[1, after % 4], (after // 4, 4 * q + r))
        for r in range(4)
    ]
    for args in rel_args:
        push(*args)

    @pl.loop(GROUPS, 2 * GROUPS)
    def _(g):
        group(g, False)

    early = after < 4

    def give_residual():
        for args in res_args:
            push(*args)

    pl.when(early)(give_residual)

    con_local.wait()
    pl.when(has_cl)(lambda: to_cr.wait_recv())
    pl.when(has_cr)(lambda: to_cl.wait_recv())

    def chain_fill(layer):
        cond = natural(con_nat, layer)
        for n in range(3):
            kappa = cond * (1.0 / COARSE_ROOTS[n])
            kc[n, layer] = kappa
            mc[n, layer] = 1.0 - 6.0 * kappa

    for layer in range(CH, CH + 4):
        chain_fill(layer)
    for has, first in ((has_cl, 0), (has_cr, CH + 4)):
        @pl.when(has)
        def _(first=first):
            for layer in range(first, first + CH):
                chain_fill(layer)

        @pl.when(jnp.logical_not(has))
        def _(first=first):
            for layer in range(first, first + CH):
                for n in range(3):
                    kc[n, layer] = nothing
                    mc[n, layer] = nothing
                eb[0, layer] = nothing
                eb[1, layer] = nothing

    def out_rows(ref, i, layer, value):
        for j in range(8):
            ref[i, layer, pl.ds(j, 8, stride=8), :] = value[j]

    def chain_copies(i):
        p = i % 2
        core = jnp.where(i == 3, 1, m)
        lft, rgt = (core, c - 1), (core, c + 1)
        return (
            remote(eb.at[p, pl.ds(CH, CH)], eb.at[p, pl.ds(CH + 4, CH)], chain_send.at[0, p], chain_recv.at[0, p], lft),
            remote(eb.at[p, pl.ds(4, CH)], eb.at[p, pl.ds(0, CH)], chain_send.at[1, p], chain_recv.at[1, p], rgt),
        )

    over = remote(eb.at[1, pl.ds(CH, 4)], eb.at[1, pl.ds(CH, 4)], chain_send.at[2, 0], chain_recv.at[2, 0], (1, c))

    @pl.when(m == 1)
    def _():
        pl.semaphore_wait(turn, 1)
        pl.when(jnp.logical_not(early))(give_residual)

    @pl.loop(0, 4)
    def _(i):
        p = i % 2
        o = 1 - p
        arrived(res_in.at[i], out_recv.at[1, i])
        start = jnp.logical_and(m == 0, i == 0)

        @pl.when(start)
        def _():
            for layer in range(4):
                eb[p, CH + layer] = res_in[i, layer]

        @pl.when(jnp.logical_not(start))
        def _():
            a, b = chain_copies(i + 1)
            pl.when(has_cr)(lambda: a.wait_recv())
            pl.when(has_cl)(lambda: b.wait_recv())
            pl.when(i == 0)(lambda: over.wait_recv())

            @pl.when(i >= 2)
            def _():
                d, e = chain_copies(i - 2)
                pl.when(has_cl)(lambda: d.wait_send())
                pl.when(has_cr)(lambda: e.wait_send())

            src = eb.at[o]
            for n, dst in enumerate((t1, t2, None)):
                for layer in range(n + 1, CT - n - 1):
                    centre = src[layer]
                    total = neighbours(src[layer - 1], centre, src[layer + 1], mk)
                    value = mc[n, layer] * centre + kc[n, layer] * total
                    if dst is None:
                        eb[p, layer] = value + res_in[i, layer - CH]
                    else:
                        dst[layer] = value
                src = dst

        d, e = chain_copies(i)
        more = jnp.logical_or(i < 3, m == 0)
        pl.when(jnp.logical_and(more, has_cl))(lambda: d.start())
        pl.when(jnp.logical_and(more, has_cr))(lambda: e.start())
        pl.when(jnp.logical_and(i == 3, m == 0))(lambda: over.start())

        @pl.when(jnp.logical_and(i == 0, m == 0))
        def _():
            pl.semaphore_signal(turn, inc=1, device_id=(1, c), device_id_type=MESH)
            pl.when(jnp.logical_not(early))(give_residual)

        arrived(rel_in.at[i], out_recv.at[0, i])
        for layer in range(4):
            out_rows(residual, i, layer, res_in[i, layer])
            out_rows(corrected, i, layer, rel_in[i, layer] + eb[p, CH + layer])

    d, e = chain_copies(2)
    pl.when(has_cl)(lambda: d.wait_send())
    pl.when(has_cr)(lambda: e.wait_send())
    d, e = chain_copies(3)

    @pl.when(m == 0)
    def _():
        pl.when(has_cl)(lambda: d.wait_send())
        pl.when(has_cr)(lambda: e.wait_send())
        over.wait_send()

    for args, when in sends:
        if when is None:
            pushed(*args)
        else:
            pl.when(when)(lambda: pushed(*args))
    pl.when(m == 0)(lambda: pushed(initial, nat.at[1, place], in_send.at[1, 4], in_recv.at[1, sr], device(0, sq)))
    for array in (0, 2):
        for relay in relays[array]:
            relay.wait_send()
    sub.wait_send()
    for to_l, to_r in nat_copies:
        pl.when(has_l)(lambda: to_l.wait_send())
        pl.when(has_r)(lambda: to_r.wait_send())
    pl.when(has_cl)(lambda: to_cl.wait_send())
    pl.when(has_cr)(lambda: to_cr.wait_send())
    to_partner.wait_send()
    for args in rel_args + res_args:
        pushed(*args)
    a, b = state_copies(2 * GROUPS - 1)
    pl.when(has_l)(lambda: a.wait_send())
    pl.when(has_r)(lambda: b.wait_send())


def body(initial, guess, conduct, source, profile):
    amount = jnp.broadcast_to(profile[:, None], (4 * COARSEN, 128))
    anyspace = pl.BlockSpec(memory_space=pl.ANY)
    vmem = pl.BlockSpec(memory_space=pltpu.VMEM)
    out = jax.ShapeDtypeStruct((4, 4, 64, 128), F32)
    dma = pltpu.SemaphoreType.DMA

    def layers(*lead):
        return pltpu.VMEM((*lead, 8, 8, 128), F32)

    return pl.pallas_call(
        kernel,
        name="mgrit",
        out_shape=(out, out),
        in_specs=[anyspace, anyspace, anyspace, anyspace, vmem],
        out_specs=(vmem, vmem),
        scratch_shapes=[
            pltpu.VMEM((4, LT, 64, 128), F32),
            pltpu.VMEM((CT, 64, 128), F32),
            pltpu.VMEM((2, 4 * COARSEN, 128), F32),
            layers(4, LT),
            layers(3, LT),
            layers(LT),
            layers(LT),
            layers(LT),
            layers(2, 2, H),
            layers(2, 2, H),
            layers(B),
            layers(3, CT),
            layers(3, CT),
            layers(2, CT),
            layers(CT),
            layers(CT),
            layers(4, 4),
            layers(4, 4),
            dma((4, 5)), dma((4, 4)),
            dma((2, 3)), dma((2, 3)),
            dma((2,)), dma((5,)), dma((2,)),
            dma((2, 2)), dma((2, 2)),
            dma((2, 4)), dma((2, 4)),
            dma((3, 2)), dma((3, 2)), pltpu.SemaphoreType.REGULAR,
        ],
        compiler_params=pltpu.CompilerParams(
            collective_id=0, has_side_effects=True, vmem_limit_bytes=67043328
        ),
    )(initial, guess, conduct, source, amount)


def solution(mesh):
    return jax.shard_map(
        body,
        mesh=mesh,
        in_specs=(
            P("space", None, None),
            P("tm", "space", None, None),
            P("space", None, None),
            P("space", None, None),
            P("tm"),
        ),
        out_specs=(P("tm", "space", None, None), P("tm", "space", None, None)),
        check_vma=False,
    )
```

```python
import numpy as np
import jax
import jax.numpy as jnp
from jax import lax
from jax.experimental import pallas as pl
from jax.experimental.pallas import tpu as pltpu
from jax.sharding import PartitionSpec as P

SWEEPS = 3
KAPPA_TOP = 3.0
COARSEN = 8
H = 6
B = 16
LT = B + 2 * H
GROUPS = COARSEN * SWEEPS // H
CH = 3
CT = 4 + 2 * CH
F32 = jnp.float32
MESH = pl.DeviceIdType.MESH


def polynomials(scale, top):
    middle, spread = (top + 1.0) / 2.0, (top - 1.0) / 2.0
    relative = middle / spread
    ratio = 1.0 / relative
    one = np.polynomial.Polynomial([1.0])
    system = np.polynomial.Polynomial([1.0, scale])
    remain = one
    update = remain / middle
    total = update
    for _ in range(SWEEPS - 1):
        remain = remain - system * update
        following = 1.0 / (2.0 * relative - ratio)
        update = following * ratio * update + 2.0 * following / spread * remain
        total = total + update
        ratio = following
    rest = one - np.polynomial.Polynomial([0.0, scale]) * total
    return [float(r) for r in np.sort(rest.roots().real)], [float(c) for c in total.coef]


FINE_ROOTS, FINE_P = polynomials(1.0, 1.0 + 12.0 * KAPPA_TOP)
COARSE_ROOTS, _ = polynomials(float(COARSEN), 1.0 + 12.0 * KAPPA_TOP * COARSEN)


class Masks:
    def __init__(self):
        lane = lax.broadcasted_iota(jnp.int32, (8, 8, 128), 2)
        sub = lax.broadcasted_iota(jnp.int32, (8, 128), 0)
        self.first_lane, self.last_lane = lane == 0, lane == 127
        self.first_sub, self.last_sub = sub == 0, sub == 7


def neighbours(below, centre, above, mk):
    side = jnp.where(mk.first_lane, 0.0, pltpu.roll(centre, 1, 2))
    side = side + jnp.where(mk.last_lane, 0.0, pltpu.roll(centre, 127, 2))
    before = jnp.where(mk.first_sub, 0.0, pltpu.roll(centre[7], 1, 0))
    after = jnp.where(mk.last_sub, 0.0, pltpu.roll(centre[0], 7, 0))
    rows = jnp.concatenate([before[None], centre[:7]], axis=0) + jnp.concatenate(
        [centre[1:], after[None]], axis=0
    )
    return (side + rows) + (below + above)


def natural(ref, layer):
    return jnp.stack([ref[layer, pl.ds(j, 8, stride=8), :] for j in range(8)], axis=0)


def each(lo, hi, run, unroll):
    assert (hi - lo) % unroll == 0

    @pl.loop(0, (hi - lo) // unroll)
    def _(t):
        for d in range(unroll):
            run(lo + t * unroll + d)


def kernel(
    initial, guess, conduct, source, amount,
    corrected, residual,
    nat, con_nat, prof, kap, mul, grow, ua, ub, land, stage, rel, kc, mc, eb, t1, t2, res_in, rel_in,
    in_send, in_recv, nat_send, nat_recv, prof_sem, con_sem, sub_sem, halo_send, halo_recv,
    out_send, out_recv, chain_send, chain_recv, fin, fin_sem, turn,
):
    m = lax.axis_index("tm")
    c = lax.axis_index("space")
    mk = Masks()

    x, y, z = c % 4, (c // 4) % 4, c // 16
    half = y // 2
    s = jnp.where(half == 0, y, 3 - y)
    k = x + 4 * half
    q = 2 * (2 * z + (s + z) % 2) + m

    def device(kk, qq):
        b = qq // 2
        zz = b // 2
        ss = (b % 2 + zz % 2) % 2
        yy = jnp.where(kk // 4 == 0, ss, 3 - ss)
        return (qq % 2, zz * 16 + yy * 4 + kk % 4)

    def remote(src, dst, ssem, rsem, to):
        return pltpu.make_async_remote_copy(
            src_ref=src, dst_ref=dst, send_sem=ssem, recv_sem=rsem, device_id=to, device_id_type=MESH
        )

    def is_me(to):
        return jnp.logical_and(to[0] == m, to[1] == c)

    def push(src, dst, ssem, rsem, to):
        mine = is_me(to)

        @pl.when(mine)
        def _():
            pltpu.make_async_copy(src, dst, rsem).start()

        @pl.when(jnp.logical_not(mine))
        def _():
            remote(src, dst, ssem, rsem, to).start()

    def pushed(src, dst, ssem, rsem, to):
        @pl.when(jnp.logical_not(is_me(to)))
        def _():
            remote(src, dst, ssem, rsem, to).wait_send()

    def arrived(dst, rsem):
        pltpu.make_async_copy(dst, dst, rsem).wait()

    left, right = device(k, jnp.maximum(q - 1, 0)), device(k, jnp.minimum(q + 1, 15))
    has_l, has_r = q > 0, q < 15
    sq, sr = c // 4, c % 4
    has_cl, has_cr = c > 0, c < 63
    barrier = pltpu.get_barrier_semaphore()

    def hello(to):
        pl.semaphore_signal(barrier, inc=1, device_id=to, device_id_type=MESH)

    for kk in range(8):
        for to in (device(kk, sq), (kk // 4, 4 * q + kk % 4)):
            pl.when(jnp.logical_not(is_me(to)))(lambda: hello(to))
    for d in range(1, 8):
        hello(device((k + d) % 8, q))
    hello((1 - m, c))
    hello(device(k, (q + 1) % 16))
    hello(device(k, (q + 15) % 16))
    for d in (1, 63):
        hello((0, (c + d) % 64))
        hello((1, (c + d) % 64))
    pl.semaphore_wait(barrier, 30 - 2 * jnp.where(sq == q, 1, 0))

    place = pl.ds(H + 4 * sr, 4)
    own = pl.ds(H, B)
    sends = []

    def give(array, slot, src, kk, when=None):
        args = (src, nat.at[array, place], in_send.at[array, slot], in_recv.at[array, sr], device(kk, sq))
        sends.append((args, when))
        if when is None:
            push(*args)
        else:
            pl.when(when)(lambda: push(*args))

    chain_left, chain_right = (m, c - 1), (m, c + 1)
    con_local = pltpu.make_async_copy(conduct, con_nat.at[pl.ds(CH, 4)], con_sem.at[0])
    to_cl = remote(conduct.at[pl.ds(0, CH)], con_nat.at[pl.ds(CH + 4, CH)], con_sem.at[1], con_sem.at[2], chain_left)
    to_cr = remote(conduct.at[pl.ds(1, CH)], con_nat.at[pl.ds(0, CH)], con_sem.at[3], con_sem.at[4], chain_right)

    partner = (1 - m, c)
    to_partner = remote(prof.at[m], prof.at[m], prof_sem.at[0], prof_sem.at[1], partner)

    give(0, 0, conduct, x + 4 * m)
    give(2, 0, source, x + 4 * m)
    relays = {}
    for array in (0, 2):
        column = nat.at[array, pl.ds(H + 4 * x, 4)]
        relays[array] = [
            remote(column, column, in_send.at[array, d], in_recv.at[array, x], (m, 16 * z + 4 * y + (x + d) % 4)) for d in range(1, 4)
        ]
        arrived(column, in_recv.at[array, x])
        for relay in relays[array]:
            relay.start()
    pl.when(m == 0)(lambda: push(initial, nat.at[1, place], in_send.at[1, 4], in_recv.at[1, sr], device(0, sq)))
    for i in range(3):
        give(1, i, guess.at[i], 4 * m + i + 1)
    give(1, 3, guess.at[3], 4, m == 0)
    for t in range(4 * COARSEN):
        prof[m, pl.ds(t, 1), :] = jnp.full((1, 128), amount[t], F32)

    nat_copies = []

    def beside(array):
        to_l = remote(
            nat.at[array, pl.ds(H, H)], nat.at[array, pl.ds(H + B, H)],
            nat_send.at[0, array], nat_recv.at[0, array], left,
        )
        to_r = remote(
            nat.at[array, pl.ds(B, H)], nat.at[array, pl.ds(0, H)],
            nat_send.at[1, array], nat_recv.at[1, array], right,
        )
        nat_copies.append((to_l, to_r))

        def piece(r):
            def come():
                arrived(nat.at[array, pl.ds(H + 4 * r, 4)], in_recv.at[array, r])

            if array == 1:
                come()
            else:
                pl.when(x != r)(come)

        piece(0)
        piece(1)
        pl.when(has_l)(lambda: to_l.start())
        piece(2)
        piece(3)
        pl.when(has_r)(lambda: to_r.start())

    def halo_arrived(array):
        pl.when(has_r)(lambda: arrived(nat.at[array, pl.ds(H + B, H)], nat_recv.at[0, array]))
        pl.when(has_l)(lambda: arrived(nat.at[array, pl.ds(0, H)], nat_recv.at[1, array]))

    def coefficients(layer, cond):
        for n in range(3):
            kappa = cond * (1.0 / FINE_ROOTS[n])
            kap[n, layer] = kappa
            mul[n, layer] = 1.0 - 6.0 * kappa
        kap[3, layer] = cond

    nothing = jnp.zeros((8, 8, 128), F32)

    def edges(has, first, fill, blank):
        @pl.when(has)
        def _():
            each(first, first + H, fill, 3)

        @pl.when(jnp.logical_not(has))
        def _():
            each(first, first + H, blank, 3)

    def fill_con(layer):
        coefficients(layer, natural(nat.at[0], layer))

    def blank_con(layer):
        for n in range(3):
            kap[n, layer] = nothing
            mul[n, layer] = nothing
        kap[3, layer] = nothing

    def fill_src(layer):
        ub[layer] = natural(nat.at[2], layer)

    def blank_src(layer):
        ub[layer] = nothing

    beside(0)

    each(H, H + B, fill_con, 4)

    beside(2)
    beside(1)
    sub_src, sub_dst = nat.at[1, own], nat.at[3, own]
    sub = remote(sub_src, sub_dst, sub_sem.at[0], sub_sem.at[1], device((k + 7) % 8, q))
    sub.start()
    con_local.start()
    to_partner.start()
    pl.when(has_cl)(lambda: to_cl.start())
    pl.when(has_cr)(lambda: to_cr.start())

    halo_arrived(0)
    edges(has_l, 0, fill_con, blank_con)
    edges(has_r, H + B, fill_con, blank_con)

    each(H, H + B, fill_src, 4)

    halo_arrived(2)
    edges(has_l, 0, fill_src, blank_src)
    edges(has_r, H + B, fill_src, blank_src)

    def applied(ref, layer):
        centre = ref[layer]
        return kap[3, layer] * (6.0 * centre - neighbours(ref[layer - 1], centre, ref[layer + 1], mk))

    def first_power(layer):
        ua[layer] = FINE_P[1] * ub[layer] + FINE_P[2] * applied(ub, layer)

    def second_power(layer):
        grow[layer] = FINE_P[0] * ub[layer] + applied(ua, layer)

    each(1, LT - 1, first_power, (LT - 2) // 2)
    each(2, LT - 2, second_power, (LT - 4) // 2)

    def fill_entry(layer):
        ua[layer] = natural(nat.at[1], layer)

    each(H, H + B, fill_entry, 4)

    def entry_halo(side, has, first, sem):
        def fill(layer):
            land[0, side, layer - first] = natural(nat.at[1], layer)

        def blank(layer):
            land[0, side, layer - first] = nothing
            land[1, side, layer - first] = nothing

        pl.when(has)(lambda: arrived(nat.at[1, pl.ds(first, H)], sem))
        edges(has, first, fill, blank)

    arrived(prof.at[1 - m], prof_sem.at[1])

    def state_copies(t):
        p = t % 2
        return (
            remote(stage.at[p, 0], land.at[p, 1], halo_send.at[0, p], halo_recv.at[0, p], left),
            remote(stage.at[p, 1], land.at[p, 0], halo_send.at[1, p], halo_recv.at[1, p], right),
        )

    def group(g, with_source):
        parity = g % 2
        following = (g + 1) % 2
        bufs = (ua, ub)

        def read(i, layer):
            if i == 0 and layer < H:
                return land[parity, 0, layer]
            if i == 0 and layer >= H + B:
                return land[parity, 1, layer - H - B]
            return bufs[i % 2][layer]

        amounts = {}
        if with_source:
            for n in range(H // 3):
                row = prof[k // 4, pl.ds(COARSEN * (k % 4) + g * (H // 3) + n, 1), :]
                amounts[3 * n + 3] = jnp.broadcast_to(row, (8, 128))

        def region(bounds, sent=None):
            todo = []
            for i in range(1, H + 1):
                lo, hi = bounds(i)
                todo += [(layer + 2 * i, i, layer) for layer in range(lo, hi)]
            for _, i, layer in sorted(todo):
                n = (i - 1) % 3
                centre = read(i - 1, layer)
                total = neighbours(read(i - 1, layer - 1), centre, read(i - 1, layer + 1), mk)
                value = mul[n, layer] * centre + kap[n, layer] * total
                if i in amounts:
                    value = value + amounts[i][None] * grow[layer]
                bufs[i % 2][layer] = value
                if i == H and sent is not None:
                    stage[following, sent[0], layer - sent[1]] = value

        @pl.when(g >= 2)
        def _():
            a, b = state_copies(g + 1)
            pl.when(has_l)(lambda: a.wait_send())
            pl.when(has_r)(lambda: b.wait_send())

        region(lambda i: (H + i, H + B - i))
        a, b = state_copies(g)
        c_, d_ = state_copies(g + 1)
        last = COARSEN * SWEEPS // H

        if with_source:
            pl.when(g == 0)(lambda: entry_halo(0, has_l, 0, nat_recv.at[1, 1]))

        @pl.when(jnp.logical_and(g > 0, has_l))
        def _():
            b.wait_recv()

        region(lambda i: (i, H + i), (0, H))

        @pl.when(jnp.logical_and((g + 1) % last != 0, has_l))
        def _():
            c_.start()

        if with_source:
            pl.when(g == 0)(lambda: entry_halo(1, has_r, H + B, nat_recv.at[0, 1]))

        @pl.when(jnp.logical_and(g > 0, has_r))
        def _():
            a.wait_recv()

        region(lambda i: (LT - H - i, LT - i), (1, B))

        @pl.when(jnp.logical_and((g + 1) % last != 0, has_r))
        def _():
            d_.start()

    @pl.loop(0, GROUPS)
    def _(g):
        group(g, True)

    arrived(sub_dst, sub_sem.at[1])
    first_copies = state_copies(GROUPS)
    final = k == 7

    def difference(layer):
        value = ua[layer]
        off = natural(nat.at[3], layer)
        rel[layer - H] = value
        value = jnp.where(final, off, value) - off
        ua[layer] = value
        return value

    def difference_l(i):
        stage[GROUPS % 2, 0, i] = difference(H + i)

    each(0, H, difference_l, 3)

    pl.when(has_l)(lambda: first_copies[0].start())

    def difference_r(i):
        stage[GROUPS % 2, 1, i] = difference(B + i)

    each(0, H, difference_r, 3)
    pl.when(has_r)(lambda: first_copies[1].start())
    each(2 * H, B, difference, B - 2 * H)

    after = (k + 1) % 8
    rel_args = [
        (rel.at[pl.ds(4 * r, 4)], rel_in.at[k % 4], out_send.at[0, r], out_recv.at[0, k % 4], (k // 4, 4 * q + r))
        for r in range(4)
    ]
    res_args = [
        (ua.at[pl.ds(H + 4 * r, 4)], res_in.at[after % 4], out_send.at[1, r], out_recv.at[1, after % 4], (after // 4, 4 * q + r))
        for r in range(4)
    ]
    for args in rel_args:
        push(*args)

    @pl.loop(GROUPS, 2 * GROUPS)
    def _(g):
        group(g, False)

    early = after < 4

    def give_residual():
        for args in res_args:
            push(*args)

    pl.when(early)(give_residual)

    con_local.wait()
    pl.when(has_cl)(lambda: to_cr.wait_recv())
    pl.when(has_cr)(lambda: to_cl.wait_recv())

    def chain_fill(layer):
        cond = natural(con_nat, layer)
        for n in range(3):
            kappa = cond * (1.0 / COARSE_ROOTS[n])
            kc[n, layer] = kappa
            mc[n, layer] = 1.0 - 6.0 * kappa

    for layer in range(CH, CH + 4):
        chain_fill(layer)
    for has, first in ((has_cl, 0), (has_cr, CH + 4)):
        @pl.when(has)
        def _(first=first):
            for layer in range(first, first + CH):
                chain_fill(layer)

        @pl.when(jnp.logical_not(has))
        def _(first=first):
            for layer in range(first, first + CH):
                for n in range(3):
                    kc[n, layer] = nothing
                    mc[n, layer] = nothing
                eb[0, layer] = nothing
                eb[1, layer] = nothing

    def out_rows(ref, i, layer, value):
        for j in range(8):
            ref[i, layer, pl.ds(j, 8, stride=8), :] = value[j]

    def chain_copies(i):
        p = i % 2
        core = jnp.where(i == 3, 1, m)
        lft, rgt = (core, c - 1), (core, c + 1)
        return (
            remote(eb.at[p, pl.ds(CH, CH)], eb.at[p, pl.ds(CH + 4, CH)], chain_send.at[0, p], chain_recv.at[0, p], lft),
            remote(eb.at[p, pl.ds(4, CH)], eb.at[p, pl.ds(0, CH)], chain_send.at[1, p], chain_recv.at[1, p], rgt),
        )

    def result(n, i):
        return pltpu.make_async_copy(fin.at[n, i], (corrected, residual)[n].at[i], fin_sem.at[n, i])

    over = remote(eb.at[1, pl.ds(CH, 4)], eb.at[1, pl.ds(CH, 4)], chain_send.at[2, 0], chain_recv.at[2, 0], (1, c))

    @pl.when(m == 1)
    def _():
        pl.semaphore_wait(turn, 1)
        pl.when(jnp.logical_not(early))(give_residual)

    @pl.loop(0, 4)
    def _(i):
        p = i % 2
        o = 1 - p
        arrived(res_in.at[i], out_recv.at[1, i])
        start = jnp.logical_and(m == 0, i == 0)

        @pl.when(start)
        def _():
            for layer in range(4):
                eb[p, CH + layer] = res_in[i, layer]

        @pl.when(jnp.logical_not(start))
        def _():
            a, b = chain_copies(i + 1)
            pl.when(has_cr)(lambda: a.wait_recv())
            pl.when(has_cl)(lambda: b.wait_recv())
            pl.when(i == 0)(lambda: over.wait_recv())

            @pl.when(i >= 2)
            def _():
                d, e = chain_copies(i - 2)
                pl.when(has_cl)(lambda: d.wait_send())
                pl.when(has_cr)(lambda: e.wait_send())

            src = eb.at[o]
            for n, dst in enumerate((t1, t2, None)):
                for layer in range(n + 1, CT - n - 1):
                    centre = src[layer]
                    total = neighbours(src[layer - 1], centre, src[layer + 1], mk)
                    value = mc[n, layer] * centre + kc[n, layer] * total
                    if dst is None:
                        eb[p, layer] = value + res_in[i, layer - CH]
                    else:
                        dst[layer] = value
                src = dst

        d, e = chain_copies(i)
        more = jnp.logical_or(i < 3, m == 0)
        pl.when(jnp.logical_and(more, has_cl))(lambda: d.start())
        pl.when(jnp.logical_and(more, has_cr))(lambda: e.start())
        pl.when(jnp.logical_and(i == 3, m == 0))(lambda: over.start())

        @pl.when(jnp.logical_and(i == 0, m == 0))
        def _():
            pl.semaphore_signal(turn, inc=1, device_id=(1, c), device_id_type=MESH)
            pl.when(jnp.logical_not(early))(give_residual)

        arrived(rel_in.at[i], out_recv.at[0, i])
        for layer in range(4):
            out_rows(fin.at[0], i, layer, rel_in[i, layer] + eb[p, CH + layer])
        result(0, i).start()
        for layer in range(4):
            out_rows(fin.at[1], i, layer, res_in[i, layer])
        result(1, i).start()

    for i in range(4):
        for n in range(2):
            result(n, i).wait()
    d, e = chain_copies(2)
    pl.when(has_cl)(lambda: d.wait_send())
    pl.when(has_cr)(lambda: e.wait_send())
    d, e = chain_copies(3)

    @pl.when(m == 0)
    def _():
        pl.when(has_cl)(lambda: d.wait_send())
        pl.when(has_cr)(lambda: e.wait_send())
        over.wait_send()

    for args, when in sends:
        if when is None:
            pushed(*args)
        else:
            pl.when(when)(lambda: pushed(*args))
    pl.when(m == 0)(lambda: pushed(initial, nat.at[1, place], in_send.at[1, 4], in_recv.at[1, sr], device(0, sq)))
    for array in (0, 2):
        for relay in relays[array]:
            relay.wait_send()
    sub.wait_send()
    for to_l, to_r in nat_copies:
        pl.when(has_l)(lambda: to_l.wait_send())
        pl.when(has_r)(lambda: to_r.wait_send())
    pl.when(has_cl)(lambda: to_cl.wait_send())
    pl.when(has_cr)(lambda: to_cr.wait_send())
    to_partner.wait_send()
    for args in rel_args + res_args:
        pushed(*args)
    a, b = state_copies(2 * GROUPS - 1)
    pl.when(has_l)(lambda: a.wait_send())
    pl.when(has_r)(lambda: b.wait_send())


def body(initial, guess, conduct, source, profile):
    anyspace = pl.BlockSpec(memory_space=pl.ANY)
    out = jax.ShapeDtypeStruct((4, 4, 64, 128), F32)
    dma = pltpu.SemaphoreType.DMA

    def layers(*lead):
        return pltpu.VMEM((*lead, 8, 8, 128), F32)

    return pl.pallas_call(
        kernel,
        name="mgrit",
        out_shape=(out, out),
        in_specs=[anyspace, anyspace, anyspace, anyspace, pl.BlockSpec(memory_space=pltpu.SMEM)],
        out_specs=(anyspace, anyspace),
        scratch_shapes=[
            pltpu.VMEM((4, LT, 64, 128), F32),
            pltpu.VMEM((CT, 64, 128), F32),
            pltpu.VMEM((2, 4 * COARSEN, 128), F32),
            layers(4, LT),
            layers(3, LT),
            layers(LT),
            layers(LT),
            layers(LT),
            layers(2, 2, H),
            layers(2, 2, H),
            layers(B),
            layers(3, CT),
            layers(3, CT),
            layers(2, CT),
            layers(CT),
            layers(CT),
            layers(4, 4),
            layers(4, 4),
            dma((4, 5)), dma((4, 4)),
            dma((2, 3)), dma((2, 3)),
            dma((2,)), dma((5,)), dma((2,)),
            dma((2, 2)), dma((2, 2)),
            dma((2, 4)), dma((2, 4)),
            dma((3, 2)), dma((3, 2)),
            pltpu.VMEM((2, 4, 4, 64, 128), F32),
            dma((2, 4)), pltpu.SemaphoreType.REGULAR,
        ],
        compiler_params=pltpu.CompilerParams(
            collective_id=0, has_side_effects=True, vmem_limit_bytes=67043328
        ),
    )(initial, guess, conduct, source, profile)


def solution(mesh):
    return jax.shard_map(
        body,
        mesh=mesh,
        in_specs=(
            P("space", None, None),
            P("tm", "space", None, None),
            P("space", None, None),
            P("space", None, None),
            P("tm"),
        ),
        out_specs=(P("tm", "space", None, None), P("tm", "space", None, None)),
        check_vma=False,
    )
```

```python
import numpy as np
import jax
import jax.numpy as jnp
from jax import lax
from jax.experimental import pallas as pl
from jax.experimental.pallas import tpu as pltpu
from jax.sharding import PartitionSpec as P

SWEEPS = 3
KAPPA_TOP = 3.0
COARSEN = 8
H = 6
B = 16
LT = B + 2 * H
GROUPS = COARSEN * SWEEPS // H
CH = 3
CT = 4 + 2 * CH
F32 = jnp.float32
MESH = pl.DeviceIdType.MESH


def polynomials(scale, top):
    middle, spread = (top + 1.0) / 2.0, (top - 1.0) / 2.0
    relative = middle / spread
    ratio = 1.0 / relative
    one = np.polynomial.Polynomial([1.0])
    system = np.polynomial.Polynomial([1.0, scale])
    remain = one
    update = remain / middle
    total = update
    for _ in range(SWEEPS - 1):
        remain = remain - system * update
        following = 1.0 / (2.0 * relative - ratio)
        update = following * ratio * update + 2.0 * following / spread * remain
        total = total + update
        ratio = following
    rest = one - np.polynomial.Polynomial([0.0, scale]) * total
    return [float(r) for r in np.sort(rest.roots().real)], [float(c) for c in total.coef]


FINE_ROOTS, FINE_P = polynomials(1.0, 1.0 + 12.0 * KAPPA_TOP)
COARSE_ROOTS, _ = polynomials(float(COARSEN), 1.0 + 12.0 * KAPPA_TOP * COARSEN)


class Masks:
    def __init__(self):
        lane = lax.broadcasted_iota(jnp.int32, (8, 8, 128), 2)
        sub = lax.broadcasted_iota(jnp.int32, (8, 128), 0)
        self.first_lane, self.last_lane = lane == 0, lane == 127
        self.first_sub, self.last_sub = sub == 0, sub == 7


def neighbours(below, centre, above, mk):
    side = jnp.where(mk.first_lane, 0.0, pltpu.roll(centre, 1, 2))
    side = side + jnp.where(mk.last_lane, 0.0, pltpu.roll(centre, 127, 2))
    before = jnp.where(mk.first_sub, 0.0, pltpu.roll(centre[7], 1, 0))
    after = jnp.where(mk.last_sub, 0.0, pltpu.roll(centre[0], 7, 0))
    rows = jnp.concatenate([before[None], centre[:7]], axis=0) + jnp.concatenate(
        [centre[1:], after[None]], axis=0
    )
    return (side + rows) + (below + above)


def natural(ref, layer):
    return jnp.stack([ref[layer, pl.ds(j, 8, stride=8), :] for j in range(8)], axis=0)


def each(lo, hi, run, unroll):
    assert (hi - lo) % unroll == 0

    @pl.loop(0, (hi - lo) // unroll)
    def _(t):
        for d in range(unroll):
            run(lo + t * unroll + d)


def kernel(
    initial, guess, conduct, source, amount,
    corrected, residual,
    nat, con_nat, prof, kap, mul, grow, ua, ub, land, stage, rel, kc, mc, eb, t1, t2, res_in, rel_in,
    in_send, in_recv, nat_send, nat_recv, prof_sem, con_sem, sub_sem, halo_send, halo_recv,
    out_send, out_recv, chain_send, chain_recv, fin, fin_sem, turn,
):
    m = lax.axis_index("tm")
    c = lax.axis_index("space")
    mk = Masks()

    x, y, z = c % 4, (c // 4) % 4, c // 16
    half = y // 2
    s = jnp.where(half == 0, y, 3 - y)
    k = x + 4 * half
    q = 2 * (2 * z + (s + z) % 2) + m

    def device(kk, qq):
        b = qq // 2
        zz = b // 2
        ss = (b % 2 + zz % 2) % 2
        yy = jnp.where(kk // 4 == 0, ss, 3 - ss)
        return (qq % 2, zz * 16 + yy * 4 + kk % 4)

    def remote(src, dst, ssem, rsem, to):
        return pltpu.make_async_remote_copy(
            src_ref=src, dst_ref=dst, send_sem=ssem, recv_sem=rsem, device_id=to, device_id_type=MESH
        )

    def is_me(to):
        return jnp.logical_and(to[0] == m, to[1] == c)

    def push(src, dst, ssem, rsem, to):
        mine = is_me(to)

        @pl.when(mine)
        def _():
            pltpu.make_async_copy(src, dst, rsem).start()

        @pl.when(jnp.logical_not(mine))
        def _():
            remote(src, dst, ssem, rsem, to).start()

    def pushed(src, dst, ssem, rsem, to):
        @pl.when(jnp.logical_not(is_me(to)))
        def _():
            remote(src, dst, ssem, rsem, to).wait_send()

    def arrived(dst, rsem):
        pltpu.make_async_copy(dst, dst, rsem).wait()

    left, right = device(k, jnp.maximum(q - 1, 0)), device(k, jnp.minimum(q + 1, 15))
    has_l, has_r = q > 0, q < 15
    sq, sr = c // 4, c % 4
    has_cl, has_cr = c > 0, c < 63
    barrier = pltpu.get_barrier_semaphore()

    def hello(to):
        pl.semaphore_signal(barrier, inc=1, device_id=to, device_id_type=MESH)

    for kk in range(8):
        for to in (device(kk, sq), (kk // 4, 4 * q + kk % 4)):
            pl.when(jnp.logical_not(is_me(to)))(lambda: hello(to))
    for d in range(1, 8):
        hello(device((k + d) % 8, q))
    hello((1 - m, c))
    hello(device(k, (q + 1) % 16))
    hello(device(k, (q + 15) % 16))
    for d in (1, 63):
        hello((0, (c + d) % 64))
        hello((1, (c + d) % 64))
    pl.semaphore_wait(barrier, 30 - 2 * jnp.where(sq == q, 1, 0))

    place = pl.ds(H + 4 * sr, 4)
    own = pl.ds(H, B)
    sends = []

    def give(array, slot, src, kk, when=None):
        args = (src, nat.at[array, place], in_send.at[array, slot], in_recv.at[array, sr], device(kk, sq))
        sends.append((args, when))
        if when is None:
            push(*args)
        else:
            pl.when(when)(lambda: push(*args))

    chain_left, chain_right = (m, c - 1), (m, c + 1)
    con_local = pltpu.make_async_copy(conduct, con_nat.at[pl.ds(CH, 4)], con_sem.at[0])
    to_cl = remote(conduct.at[pl.ds(0, CH)], con_nat.at[pl.ds(CH + 4, CH)], con_sem.at[1], con_sem.at[2], chain_left)
    to_cr = remote(conduct.at[pl.ds(1, CH)], con_nat.at[pl.ds(0, CH)], con_sem.at[3], con_sem.at[4], chain_right)

    partner = (1 - m, c)
    to_partner = remote(prof.at[m], prof.at[m], prof_sem.at[0], prof_sem.at[1], partner)

    give(0, 0, conduct, x + 4 * m)
    give(2, 0, source, x + 4 * m)
    relays = {}
    for array in (0, 2):
        column = nat.at[array, pl.ds(H + 4 * x, 4)]
        relays[array] = [
            remote(column, column, in_send.at[array, d], in_recv.at[array, x], (m, 16 * z + 4 * y + (x + d) % 4)) for d in (3, 1, 2)
        ]
        arrived(column, in_recv.at[array, x])
        for relay in relays[array]:
            relay.start()
    pl.when(m == 0)(lambda: push(initial, nat.at[1, place], in_send.at[1, 4], in_recv.at[1, sr], device(0, sq)))
    for i in range(3):
        give(1, i, guess.at[i], 4 * m + i + 1)
    give(1, 3, guess.at[3], 4, m == 0)
    for t in range(4 * COARSEN):
        prof[m, pl.ds(t, 1), :] = jnp.full((1, 128), amount[t], F32)

    nat_copies = []

    def beside(array):
        to_l = remote(
            nat.at[array, pl.ds(H, H)], nat.at[array, pl.ds(H + B, H)],
            nat_send.at[0, array], nat_recv.at[0, array], left,
        )
        to_r = remote(
            nat.at[array, pl.ds(B, H)], nat.at[array, pl.ds(0, H)],
            nat_send.at[1, array], nat_recv.at[1, array], right,
        )
        nat_copies.append((to_l, to_r))

        def piece(r):
            def come():
                arrived(nat.at[array, pl.ds(H + 4 * r, 4)], in_recv.at[array, r])

            if array == 1:
                come()
            else:
                pl.when(x != r)(come)

        piece(0)
        piece(1)
        pl.when(has_l)(lambda: to_l.start())
        piece(2)
        piece(3)
        pl.when(has_r)(lambda: to_r.start())

    def halo_arrived(array):
        pl.when(has_r)(lambda: arrived(nat.at[array, pl.ds(H + B, H)], nat_recv.at[0, array]))
        pl.when(has_l)(lambda: arrived(nat.at[array, pl.ds(0, H)], nat_recv.at[1, array]))

    def coefficients(layer, cond):
        for n in range(3):
            kappa = cond * (1.0 / FINE_ROOTS[n])
            kap[n, layer] = kappa
            mul[n, layer] = 1.0 - 6.0 * kappa
        kap[3, layer] = cond

    nothing = jnp.zeros((8, 8, 128), F32)

    def edges(has, first, fill, blank):
        @pl.when(has)
        def _():
            each(first, first + H, fill, 3)

        @pl.when(jnp.logical_not(has))
        def _():
            each(first, first + H, blank, 3)

    def fill_con(layer):
        coefficients(layer, natural(nat.at[0], layer))

    def blank_con(layer):
        for n in range(3):
            kap[n, layer] = nothing
            mul[n, layer] = nothing
        kap[3, layer] = nothing

    def fill_src(layer):
        ub[layer] = natural(nat.at[2], layer)

    def blank_src(layer):
        ub[layer] = nothing

    beside(0)

    each(H, H + B, fill_con, 4)

    beside(2)
    beside(1)
    sub_src, sub_dst = nat.at[1, own], nat.at[3, own]
    sub = remote(sub_src, sub_dst, sub_sem.at[0], sub_sem.at[1], device((k + 7) % 8, q))
    sub.start()
    con_local.start()
    to_partner.start()
    pl.when(has_cl)(lambda: to_cl.start())
    pl.when(has_cr)(lambda: to_cr.start())

    halo_arrived(0)
    edges(has_l, 0, fill_con, blank_con)
    edges(has_r, H + B, fill_con, blank_con)

    each(H, H + B, fill_src, 4)

    halo_arrived(2)
    edges(has_l, 0, fill_src, blank_src)
    edges(has_r, H + B, fill_src, blank_src)

    def applied(ref, layer):
        centre = ref[layer]
        return kap[3, layer] * (6.0 * centre - neighbours(ref[layer - 1], centre, ref[layer + 1], mk))

    def first_power(layer):
        ua[layer] = FINE_P[1] * ub[layer] + FINE_P[2] * applied(ub, layer)

    def second_power(layer):
        grow[layer] = FINE_P[0] * ub[layer] + applied(ua, layer)

    each(1, LT - 1, first_power, (LT - 2) // 2)
    each(2, LT - 2, second_power, (LT - 4) // 2)

    def fill_entry(layer):
        ua[layer] = natural(nat.at[1], layer)

    each(H, H + B, fill_entry, 4)

    def entry_halo(side, has, first, sem):
        def fill(layer):
            land[0, side, layer - first] = natural(nat.at[1], layer)

        def blank(layer):
            land[0, side, layer - first] = nothing
            land[1, side, layer - first] = nothing

        pl.when(has)(lambda: arrived(nat.at[1, pl.ds(first, H)], sem))
        edges(has, first, fill, blank)

    arrived(prof.at[1 - m], prof_sem.at[1])

    def state_copies(t):
        p = t % 2
        return (
            remote(stage.at[p, 0], land.at[p, 1], halo_send.at[0, p], halo_recv.at[0, p], left),
            remote(stage.at[p, 1], land.at[p, 0], halo_send.at[1, p], halo_recv.at[1, p], right),
        )

    def group(g, with_source):
        parity = g % 2
        following = (g + 1) % 2
        bufs = (ua, ub)

        def read(i, layer):
            if i == 0 and layer < H:
                return land[parity, 0, layer]
            if i == 0 and layer >= H + B:
                return land[parity, 1, layer - H - B]
            return bufs[i % 2][layer]

        amounts = {}
        if with_source:
            for n in range(H // 3):
                row = prof[k // 4, pl.ds(COARSEN * (k % 4) + g * (H // 3) + n, 1), :]
                amounts[3 * n + 3] = jnp.broadcast_to(row, (8, 128))

        def region(bounds, sent=None):
            todo = []
            for i in range(1, H + 1):
                lo, hi = bounds(i)
                todo += [(layer + 2 * i, i, layer) for layer in range(lo, hi)]
            for _, i, layer in sorted(todo):
                n = (i - 1) % 3
                centre = read(i - 1, layer)
                total = neighbours(read(i - 1, layer - 1), centre, read(i - 1, layer + 1), mk)
                value = mul[n, layer] * centre + kap[n, layer] * total
                if i in amounts:
                    value = value + amounts[i][None] * grow[layer]
                bufs[i % 2][layer] = value
                if i == H and sent is not None:
                    stage[following, sent[0], layer - sent[1]] = value

        @pl.when(g >= 2)
        def _():
            a, b = state_copies(g + 1)
            pl.when(has_l)(lambda: a.wait_send())
            pl.when(has_r)(lambda: b.wait_send())

        region(lambda i: (H + i, H + B - i))
        a, b = state_copies(g)
        c_, d_ = state_copies(g + 1)
        last = COARSEN * SWEEPS // H

        if with_source:
            pl.when(g == 0)(lambda: entry_halo(0, has_l, 0, nat_recv.at[1, 1]))

        @pl.when(jnp.logical_and(g > 0, has_l))
        def _():
            b.wait_recv()

        region(lambda i: (i, H + i), (0, H))

        @pl.when(jnp.logical_and((g + 1) % last != 0, has_l))
        def _():
            c_.start()

        if with_source:
            pl.when(g == 0)(lambda: entry_halo(1, has_r, H + B, nat_recv.at[0, 1]))

        @pl.when(jnp.logical_and(g > 0, has_r))
        def _():
            a.wait_recv()

        region(lambda i: (LT - H - i, LT - i), (1, B))

        @pl.when(jnp.logical_and((g + 1) % last != 0, has_r))
        def _():
            d_.start()

    @pl.loop(0, GROUPS)
    def _(g):
        group(g, True)

    arrived(sub_dst, sub_sem.at[1])
    first_copies = state_copies(GROUPS)
    final = k == 7

    def difference(layer):
        value = ua[layer]
        off = natural(nat.at[3], layer)
        rel[layer - H] = value
        value = jnp.where(final, off, value) - off
        ua[layer] = value
        return value

    def difference_l(i):
        stage[GROUPS % 2, 0, i] = difference(H + i)

    each(0, H, difference_l, 3)

    pl.when(has_l)(lambda: first_copies[0].start())

    def difference_r(i):
        stage[GROUPS % 2, 1, i] = difference(B + i)

    each(0, H, difference_r, 3)
    pl.when(has_r)(lambda: first_copies[1].start())
    each(2 * H, B, difference, B - 2 * H)

    after = (k + 1) % 8
    rel_args = [
        (rel.at[pl.ds(4 * r, 4)], rel_in.at[k % 4], out_send.at[0, r], out_recv.at[0, k % 4], (k // 4, 4 * q + r))
        for r in range(4)
    ]
    res_args = [
        (ua.at[pl.ds(H + 4 * r, 4)], res_in.at[after % 4], out_send.at[1, r], out_recv.at[1, after % 4], (after // 4, 4 * q + r))
        for r in range(4)
    ]
    for args in rel_args:
        push(*args)

    @pl.loop(GROUPS, 2 * GROUPS)
    def _(g):
        group(g, False)

    early = after < 4

    def give_residual():
        for args in res_args:
            push(*args)

    pl.when(early)(give_residual)

    con_local.wait()
    pl.when(has_cl)(lambda: to_cr.wait_recv())
    pl.when(has_cr)(lambda: to_cl.wait_recv())

    def chain_fill(layer):
        cond = natural(con_nat, layer)
        for n in range(3):
            kappa = cond * (1.0 / COARSE_ROOTS[n])
            kc[n, layer] = kappa
            mc[n, layer] = 1.0 - 6.0 * kappa

    for layer in range(CH, CH + 4):
        chain_fill(layer)
    for has, first in ((has_cl, 0), (has_cr, CH + 4)):
        @pl.when(has)
        def _(first=first):
            for layer in range(first, first + CH):
                chain_fill(layer)

        @pl.when(jnp.logical_not(has))
        def _(first=first):
            for layer in range(first, first + CH):
                for n in range(3):
                    kc[n, layer] = nothing
                    mc[n, layer] = nothing
                eb[0, layer] = nothing
                eb[1, layer] = nothing

    def out_rows(ref, i, layer, value):
        for j in range(8):
            ref[i, layer, pl.ds(j, 8, stride=8), :] = value[j]

    def chain_copies(i):
        p = i % 2
        core = jnp.where(i == 3, 1, m)
        lft, rgt = (core, c - 1), (core, c + 1)
        return (
            remote(eb.at[p, pl.ds(CH, CH)], eb.at[p, pl.ds(CH + 4, CH)], chain_send.at[0, p], chain_recv.at[0, p], lft),
            remote(eb.at[p, pl.ds(4, CH)], eb.at[p, pl.ds(0, CH)], chain_send.at[1, p], chain_recv.at[1, p], rgt),
        )

    def result(n, i):
        return pltpu.make_async_copy(fin.at[n, i], (corrected, residual)[n].at[i], fin_sem.at[n, i])

    over = remote(eb.at[1, pl.ds(CH, 4)], eb.at[1, pl.ds(CH, 4)], chain_send.at[2, 0], chain_recv.at[2, 0], (1, c))

    @pl.when(m == 1)
    def _():
        pl.semaphore_wait(turn, 1)
        pl.when(jnp.logical_not(early))(give_residual)

    @pl.loop(0, 4)
    def _(i):
        p = i % 2
        o = 1 - p
        arrived(res_in.at[i], out_recv.at[1, i])
        start = jnp.logical_and(m == 0, i == 0)

        @pl.when(start)
        def _():
            for layer in range(4):
                eb[p, CH + layer] = res_in[i, layer]

        @pl.when(jnp.logical_not(start))
        def _():
            a, b = chain_copies(i + 1)
            pl.when(has_cr)(lambda: a.wait_recv())
            pl.when(has_cl)(lambda: b.wait_recv())
            pl.when(i == 0)(lambda: over.wait_recv())

            @pl.when(i >= 2)
            def _():
                d, e = chain_copies(i - 2)
                pl.when(has_cl)(lambda: d.wait_send())
                pl.when(has_cr)(lambda: e.wait_send())

            src = eb.at[o]
            for n, dst in enumerate((t1, t2, None)):
                for layer in range(n + 1, CT - n - 1):
                    centre = src[layer]
                    total = neighbours(src[layer - 1], centre, src[layer + 1], mk)
                    value = mc[n, layer] * centre + kc[n, layer] * total
                    if dst is None:
                        eb[p, layer] = value + res_in[i, layer - CH]
                    else:
                        dst[layer] = value
                src = dst

        d, e = chain_copies(i)
        more = jnp.logical_or(i < 3, m == 0)
        pl.when(jnp.logical_and(more, has_cl))(lambda: d.start())
        pl.when(jnp.logical_and(more, has_cr))(lambda: e.start())
        pl.when(jnp.logical_and(i == 3, m == 0))(lambda: over.start())

        @pl.when(jnp.logical_and(i == 0, m == 0))
        def _():
            pl.semaphore_signal(turn, inc=1, device_id=(1, c), device_id_type=MESH)
            pl.when(jnp.logical_not(early))(give_residual)

        arrived(rel_in.at[i], out_recv.at[0, i])
        for layer in range(4):
            out_rows(fin.at[0], i, layer, rel_in[i, layer] + eb[p, CH + layer])
        result(0, i).start()
        for layer in range(4):
            out_rows(fin.at[1], i, layer, res_in[i, layer])
        result(1, i).start()

    for i in range(4):
        for n in range(2):
            result(n, i).wait()
    d, e = chain_copies(2)
    pl.when(has_cl)(lambda: d.wait_send())
    pl.when(has_cr)(lambda: e.wait_send())
    d, e = chain_copies(3)

    @pl.when(m == 0)
    def _():
        pl.when(has_cl)(lambda: d.wait_send())
        pl.when(has_cr)(lambda: e.wait_send())
        over.wait_send()

    for args, when in sends:
        if when is None:
            pushed(*args)
        else:
            pl.when(when)(lambda: pushed(*args))
    pl.when(m == 0)(lambda: pushed(initial, nat.at[1, place], in_send.at[1, 4], in_recv.at[1, sr], device(0, sq)))
    for array in (0, 2):
        for relay in relays[array]:
            relay.wait_send()
    sub.wait_send()
    for to_l, to_r in nat_copies:
        pl.when(has_l)(lambda: to_l.wait_send())
        pl.when(has_r)(lambda: to_r.wait_send())
    pl.when(has_cl)(lambda: to_cl.wait_send())
    pl.when(has_cr)(lambda: to_cr.wait_send())
    to_partner.wait_send()
    for args in rel_args + res_args:
        pushed(*args)
    a, b = state_copies(2 * GROUPS - 1)
    pl.when(has_l)(lambda: a.wait_send())
    pl.when(has_r)(lambda: b.wait_send())


def body(initial, guess, conduct, source, profile):
    anyspace = pl.BlockSpec(memory_space=pl.ANY)
    out = jax.ShapeDtypeStruct((4, 4, 64, 128), F32)
    dma = pltpu.SemaphoreType.DMA

    def layers(*lead):
        return pltpu.VMEM((*lead, 8, 8, 128), F32)

    return pl.pallas_call(
        kernel,
        name="mgrit",
        out_shape=(out, out),
        in_specs=[anyspace, anyspace, anyspace, anyspace, pl.BlockSpec(memory_space=pltpu.SMEM)],
        out_specs=(anyspace, anyspace),
        scratch_shapes=[
            pltpu.VMEM((4, LT, 64, 128), F32),
            pltpu.VMEM((CT, 64, 128), F32),
            pltpu.VMEM((2, 4 * COARSEN, 128), F32),
            layers(4, LT),
            layers(3, LT),
            layers(LT),
            layers(LT),
            layers(LT),
            layers(2, 2, H),
            layers(2, 2, H),
            layers(B),
            layers(3, CT),
            layers(3, CT),
            layers(2, CT),
            layers(CT),
            layers(CT),
            layers(4, 4),
            layers(4, 4),
            dma((4, 5)), dma((4, 4)),
            dma((2, 3)), dma((2, 3)),
            dma((2,)), dma((5,)), dma((2,)),
            dma((2, 2)), dma((2, 2)),
            dma((2, 4)), dma((2, 4)),
            dma((3, 2)), dma((3, 2)),
            pltpu.VMEM((2, 4, 4, 64, 128), F32),
            dma((2, 4)), pltpu.SemaphoreType.REGULAR,
        ],
        compiler_params=pltpu.CompilerParams(
            collective_id=0, has_side_effects=True, vmem_limit_bytes=67043328
        ),
    )(initial, guess, conduct, source, profile)


def solution(mesh):
    return jax.shard_map(
        body,
        mesh=mesh,
        in_specs=(
            P("space", None, None),
            P("tm", "space", None, None),
            P("space", None, None),
            P("space", None, None),
            P("tm"),
        ),
        out_specs=(P("tm", "space", None, None), P("tm", "space", None, None)),
        check_vma=False,
    )
```
